256 devices in a mesh: gx: 64 (over z, x, core), gy: 4 (over y).
Axes of the slice: x: 4, y: 4, z: 8, core: 2. Of those that a mesh axis runs over, the one named last changes fastest.
Arguments:
- conserved: float32 [5, 1024, 64, 512], P(None, 'gx', 'gy'), as said below
- shock_flags: int32 [64, 4, 32], P('gx', 'gy'), may hold values from 0 to 1, as said below
Outputs:
- advanced: float32 [5, 1024, 64, 512], P(None, 'gx', 'gy')
- tendency: float32 [5, 1024, 64, 512], P(None, 'gx', 'gy')
The draws below stay inside these ranges and needn't reach their ends.
Inputs may be any that keep to these rules, and one draw needn't show every extreme that they name: `shock_flags`: for every block index along the second dimension, the blocks flagged 1 lie within a quarter of the 64 block columns along the first dimension, consecutive when counted cyclically. `conserved`: density and pressure are positive in every cell.
All inputs are finite; a program needn't handle non-finite values.
Results may differ from the reference program's by a relative error of at most 0.0003.
Values sent between devices are 32-bit elements; how exact they have to be, the bound alone decides.
No kernel may reach another device: no remote copies, remote signals or barrier semaphores. Data moves between devices by JAX's collectives and lax.ppermute only.
A program may use at most 128 MiB of HBM per device.

```python
import math
import jax
import jax.numpy as jnp
from jax import lax

EDGE = 16
NB = 32
NXB = 64
NYB = 4
NX = 1024
NY = 64
NZ = 512


def draw_conserved(key, part):
    key_list = jax.random.split(key, 5)
    grid_shape = (NX, NY, NZ)
    ramp_up = 1.0 + 2.0 * jnp.arange(NX, dtype=jnp.float32)[:, None, None] / NX
    density = jnp.exp(jax.random.uniform(key_list[0], grid_shape, jnp.float32, math.log(0.5), math.log(2.0)))
    velocities = [0.5 * jax.random.truncated_normal(key_list[1 + direction], -3.0, 3.0, grid_shape, jnp.float32) for direction in range(3)]
    pressure = ramp_up * jax.random.uniform(key_list[4], grid_shape, jnp.float32, 0.5, 1.5)
    kinetic = 0.5 * density * (velocities[0] * velocities[0] + velocities[1] * velocities[1] + velocities[2] * velocities[2])
    return jnp.stack([density, density * velocities[0], density * velocities[1], density * velocities[2], pressure / 0.4 + kinetic]).astype(jnp.float32)


def draw_shock_flags(key, part):
    key_list = jax.random.split(key, 2)
    starts = jax.random.randint(key_list[0], (NYB,), 0, NXB)
    columns = jnp.arange(NXB, dtype=jnp.int32)[:, None]
    inside = (columns - starts[None, :]) % NXB < NXB // 4
    coins = jax.random.randint(key_list[1], (NXB, NYB, NB), 0, 4)
    return jnp.where(inside[:, :, None] & (coins > 0), 1, 0).astype(jnp.int32)


def setup_inputs(seed: int = 0) -> dict:
    streams_of = jax.random.split(jax.random.key(seed), 3)
    return {
        "conserved": draw_conserved(jax.random.fold_in(streams_of[2], 71), 0),
        "shock_flags": draw_shock_flags(jax.random.fold_in(streams_of[2], 71), 0),
    }


GAMMA = 1.4
GAMMA_LESS = 0.4
COURANT = 0.4
EPSILON = 1e-06

def pressure_of(density, mom_one, mom_two, mom_three, energy):
    return GAMMA_LESS * (energy - 0.5 * (mom_one * mom_one + mom_two * mom_two + mom_three * mom_three) / density)

def speed_max(fields):
    density = fields[0]
    pressure = pressure_of(density, fields[1], fields[2], fields[3], fields[4])
    sound_speed = jnp.sqrt(GAMMA * pressure / density)
    speed_sum = jnp.abs(fields[1] / density) + sound_speed + (jnp.abs(fields[2] / density) + sound_speed) + (jnp.abs(fields[3] / density) + sound_speed)
    return jnp.max(speed_sum)

def cell_flux(density, momenta, energy, normal):
    pressure = pressure_of(density, momenta[0], momenta[1], momenta[2], energy)
    velocity = momenta[normal] / density
    fluxes = [momenta[normal]]
    for other in range(3):
        if other == normal:
            fluxes.append(momenta[other] * velocity + pressure)
        else:
            fluxes.append(momenta[other] * velocity)
    fluxes.append((energy + pressure) * velocity)
    return (fluxes, pressure, velocity)

def central_line(fields, normal):
    density = fields[0]
    fluxes, pressure, velocity = cell_flux(density, [fields[1], fields[2], fields[3]], fields[4], normal)
    faces_count = density.shape[normal] - 5

    def offset(values, shift_by):
        return lax.slice_in_dim(values, shift_by, shift_by + faces_count, axis=normal)
    result = []
    for values in fluxes:
        face_flux = (offset(values, 0) + offset(values, 5) - 8.0 * (offset(values, 1) + offset(values, 4)) + 37.0 * (offset(values, 2) + offset(values, 3))) / 60.0
        result.append(lax.slice_in_dim(face_flux, 1, faces_count, axis=normal) - lax.slice_in_dim(face_flux, 0, faces_count - 1, axis=normal))
    return jnp.stack(result)

def central_div(padded):
    size_one = padded.shape[1] - 6
    size_two = padded.shape[2] - 6
    size_three = padded.shape[3] - 6
    along_one = padded[:, :, 3:3 + size_two, 3:3 + size_three]
    along_two = padded[:, 3:3 + size_one, :, 3:3 + size_three]
    along_three = padded[:, 3:3 + size_one, 3:3 + size_two, :]
    return central_line(along_one, 0) + central_line(along_two, 1) + central_line(along_three, 2)

def weno_five(far_left, near_left, centre, near_right, far_right):
    first_guess = (2.0 * far_left - 7.0 * near_left + 11.0 * centre) / 6.0
    second_guess = (-near_left + 5.0 * centre + 2.0 * near_right) / 6.0
    third_guess = (2.0 * centre + 5.0 * near_right - far_right) / 6.0
    smooth_one = 13.0 / 12.0 * (far_left - 2.0 * near_left + centre) ** 2 + 0.25 * (far_left - 4.0 * near_left + 3.0 * centre) ** 2
    smooth_two = 13.0 / 12.0 * (near_left - 2.0 * centre + near_right) ** 2 + 0.25 * (near_left - near_right) ** 2
    smooth_three = 13.0 / 12.0 * (centre - 2.0 * near_right + far_right) ** 2 + 0.25 * (3.0 * centre - 4.0 * near_right + far_right) ** 2
    weight_one = 0.1 / (EPSILON + smooth_one) ** 2
    weight_two = 0.6 / (EPSILON + smooth_two) ** 2
    weight_three = 0.3 / (EPSILON + smooth_three) ** 2
    return (weight_one * first_guess + weight_two * second_guess + weight_three * third_guess) / (weight_one + weight_two + weight_three)

def weno_lines(lines):
    faces_count = lines.shape[1] - 5
    density = lines[0]
    fluxes, pressure, velocity = cell_flux(density, [lines[1], lines[2], lines[3]], lines[4], 0)
    sound_speed = jnp.sqrt(GAMMA * pressure / density)
    enthalpy = (lines[4] + pressure) / density
    vel_two = lines[2] / density
    vel_three = lines[3] / density

    def offset(values, shift_by):
        return values[shift_by:shift_by + faces_count]
    wave_speed = jnp.abs(velocity) + sound_speed
    alpha_face = offset(wave_speed, 0)
    for shift_by in range(1, 6):
        alpha_face = jnp.maximum(alpha_face, offset(wave_speed, shift_by))
    mean_one = 0.5 * (offset(velocity, 2) + offset(velocity, 3))
    mean_two = 0.5 * (offset(vel_two, 2) + offset(vel_two, 3))
    mean_three = 0.5 * (offset(vel_three, 2) + offset(vel_three, 3))
    mean_enth = 0.5 * (offset(enthalpy, 2) + offset(enthalpy, 3))
    kinetic = 0.5 * (mean_one * mean_one + mean_two * mean_two + mean_three * mean_three)
    sound_sq = GAMMA_LESS * (mean_enth - kinetic)
    mean_sound = jnp.sqrt(sound_sq)
    inv_sound = 1.0 / mean_sound
    coef_one = GAMMA_LESS / sound_sq
    coef_two = coef_one * kinetic
    left_first = [0.5 * (coef_two + mean_one * inv_sound), -0.5 * (coef_one * mean_one + inv_sound), -0.5 * coef_one * mean_two, -0.5 * coef_one * mean_three, 0.5 * coef_one]
    left_second = [1.0 - coef_two, coef_one * mean_one, coef_one * mean_two, coef_one * mean_three, -coef_one]
    left_last = [0.5 * (coef_two - mean_one * inv_sound), -0.5 * (coef_one * mean_one - inv_sound), -0.5 * coef_one * mean_two, -0.5 * coef_one * mean_three, 0.5 * coef_one]

    def project(split_flux):
        waves = []
        waves.append(left_first[0] * split_flux[0] + left_first[1] * split_flux[1] + left_first[2] * split_flux[2] + left_first[3] * split_flux[3] + left_first[4] * split_flux[4])
        waves.append(left_second[0] * split_flux[0] + left_second[1] * split_flux[1] + left_second[2] * split_flux[2] + left_second[3] * split_flux[3] + left_second[4] * split_flux[4])
        waves.append(split_flux[2] - mean_two * split_flux[0])
        waves.append(split_flux[3] - mean_three * split_flux[0])
        waves.append(left_last[0] * split_flux[0] + left_last[1] * split_flux[1] + left_last[2] * split_flux[2] + left_last[3] * split_flux[3] + left_last[4] * split_flux[4])
        return waves
    plus_waves = []
    minus_waves = []
    for shift_by in range(6):
        state_part = [offset(lines[component], shift_by) for component in range(5)]
        flux_part = [offset(fluxes[component], shift_by) for component in range(5)]
        plus_waves.append(project([0.5 * (flux_part[component] + alpha_face * state_part[component]) for component in range(5)]))
        minus_waves.append(project([0.5 * (flux_part[component] - alpha_face * state_part[component]) for component in range(5)]))
    totals = []
    for channel in range(5):
        upwind = weno_five(plus_waves[0][channel], plus_waves[1][channel], plus_waves[2][channel], plus_waves[3][channel], plus_waves[4][channel])
        downwind = weno_five(minus_waves[5][channel], minus_waves[4][channel], minus_waves[3][channel], minus_waves[2][channel], minus_waves[1][channel])
        totals.append(upwind + downwind)
    shared = totals[0] + totals[1] + totals[4]
    faces = [shared, (mean_one - mean_sound) * totals[0] + mean_one * totals[1] + (mean_one + mean_sound) * totals[4], mean_two * shared + totals[2], mean_three * shared + totals[3], (mean_enth - mean_one * mean_sound) * totals[0] + kinetic * totals[1] + mean_two * totals[2] + mean_three * totals[3] + (mean_enth + mean_one * mean_sound) * totals[4]]
    return jnp.stack(faces)

def weno_div(block_cells):
    edge_cells = block_cells.shape[1] - 6
    along_one = block_cells[:, :, 3:3 + edge_cells, 3:3 + edge_cells]
    along_two = jnp.transpose(block_cells[:, 3:3 + edge_cells, :, 3:3 + edge_cells], (0, 2, 1, 3))
    along_three = jnp.transpose(block_cells[:, 3:3 + edge_cells, 3:3 + edge_cells, :], (0, 3, 1, 2))
    total_div = None
    for normal, lines, reverse_order in ((0, along_one, (0, 1, 2, 3)), (1, along_two, (0, 2, 1, 3)), (2, along_three, (0, 2, 3, 1))):
        order = [0, 1 + normal] + [1 + other for other in range(3) if other != normal] + [4]
        flat_lines = lines.reshape(5, edge_cells + 6, edge_cells * edge_cells)
        faces = weno_lines(jnp.stack([flat_lines[position] for position in order]))
        differences = faces[:, 1:] - faces[:, :-1]
        restored = [None] * 5
        for position, component in enumerate(order):
            restored[component] = differences[position]
        div_part = jnp.transpose(jnp.stack(restored).reshape(5, edge_cells, edge_cells, edge_cells), reverse_order)
        total_div = div_part if total_div is None else total_div + div_part
    return total_div

def empty_div(block_cells):
    edge_cells = block_cells.shape[1] - 6
    return jnp.zeros((5, edge_cells, edge_cells, edge_cells), jnp.float32)

def reference(conserved, shock_flags):
    padded = jnp.pad(conserved, ((0, 0), (3, 3), (3, 3), (3, 3)), mode='wrap')
    central = central_div(padded)
    block_total = NXB * NYB * NB

    def one_block(position):
        index_one = position // (NYB * NB)
        index_two = position // NB % NYB
        index_three = position % NB
        block_cells = lax.dynamic_slice(padded, (jnp.int32(0), index_one * EDGE, index_two * EDGE, index_three * EDGE), (5, EDGE + 6, EDGE + 6, EDGE + 6))
        return lax.cond(shock_flags[index_one, index_two, index_three] > 0, weno_div, empty_div, block_cells)
    blocks = lax.map(one_block, jnp.arange(block_total, dtype=jnp.int32))
    weno_grid = blocks.reshape(NXB, NYB, NB, 5, EDGE, EDGE, EDGE).transpose(3, 0, 4, 1, 5, 2, 6).reshape(5, NX, NY, NZ)
    shock_cells = jnp.broadcast_to(shock_flags[:, None, :, None, :, None] > 0, (NXB, EDGE, NYB, EDGE, NB, EDGE)).reshape(NX, NY, NZ)
    divergence = jnp.where(shock_cells, weno_grid, central)
    tendency = -divergence
    step_size = COURANT / speed_max(conserved)
    advanced = conserved + step_size * tendency
    return (advanced, tendency)
```

```python
import functools

import jax
import jax.numpy as jnp
from jax import lax
from jax.experimental import pallas as pl
from jax.experimental.pallas import tpu as pltpu
from jax.sharding import PartitionSpec as P

GAMMA = 1.4
GAMMA_LESS = 0.4
COURANT = 0.4
EPSILON = 1e-06
LANES = 128
ROWS = 8


def inverse(value):
    guess = pltpu.reciprocal(value, approx=True)
    return guess * (2.0 - value * guess)


def cell_values(density, mom, energy):
    inv = inverse(density)
    inv_half = 0.5 * inv
    half_vel = [m * inv_half for m in mom]
    kinetic = mom[0] * half_vel[0] + mom[1] * half_vel[1] + mom[2] * half_vel[2]
    pressure = GAMMA_LESS * (energy - kinetic)
    total = energy + pressure
    half_enth = total * inv_half
    sound = jnp.sqrt(GAMMA * pressure * inv)
    return half_vel, half_enth, pressure, total, sound


def half_flux(mom, half_vel, pressure, total, normal):
    half_normal = half_vel[normal]
    flux = [0.5 * mom[normal]]
    for other in range(3):
        part = mom[other] * half_normal
        flux.append(part + 0.5 * pressure if other == normal else part)
    flux.append(total * half_normal)
    return flux


def pair_order(normal):
    return [normal] + [other for other in range(3) if other != normal]


def recon_rest(d1, d2, d3, d4):
    t1 = d2 - d1
    t2 = d3 - d2
    t3 = d4 - d3
    d2s = 0.75 * d2
    d3s = 0.75 * d3
    b0 = t1 * t1 + d2s * (d2 + t1) + 0.75 * EPSILON
    b1 = t2 * t2 + d2s * d3 + 0.75 * EPSILON
    b2 = t3 * t3 + d3s * (d3 - t3) + 0.75 * EPSILON
    r0 = inverse(b0)
    r1 = inverse(b1)
    r2 = inverse(b2)
    z0 = r0 * r0
    z1 = r1 * r1
    z2 = 1.5 * (r2 * r2)
    num = z0 * (t2 - t1) + z2 * (t3 - t2)
    den = z2 + (0.5 * z0 + 3.0 * z1)
    return num * inverse(den)


def central_rest(d_flux):
    return [
        (1.0 / 30.0) * ((d_flux[4][c] - d_flux[0][c]) - 7.0 * (d_flux[3][c] - d_flux[1][c]))
        for c in range(5)
    ]


def weno_rest(d_flux, d_state, mean, alpha, normal):
    order = [0] + [1 + n for n in pair_order(normal)] + [4]
    a, b, e, h = mean
    twice_k = a * a + b * b + e * e
    k = 0.5 * twice_k
    s_sq = GAMMA_LESS * (h - k)
    inv_s = lax.rsqrt(s_sq)
    s = s_sq * inv_s
    half_g = (0.5 * GAMMA_LESS) * (inv_s * inv_s)
    half_inv = 0.5 * inv_s

    def project(x):
        x1 = x[1] - a * x[0]
        x2 = x[2] - b * x[0]
        x3 = x[3] - e * x[0]
        y = half_g * (x[4] - a * x1 - b * x2 - e * x3 - k * x[0])
        z = half_inv * x1
        return [y - z, x[0] - (y + y), x2, x3, y + z]

    up = []
    down = []
    for step in range(5):
        scaled = [alpha * d_state[step][c] for c in order]
        flux = [d_flux[step][c] for c in order]
        up.append([f + q for f, q in zip(flux, scaled)] if step < 4 else None)
        down.append([f - q for f, q in zip(flux, scaled)] if step > 0 else None)
    linear = [(up[1][c] - down[3][c]) - (up[2][c] - down[2][c]) for c in range(5)]
    up = [project(x) if x is not None else None for x in up]
    down = [project(x) if x is not None else None for x in down]
    t = [
        recon_rest(up[0][c], up[1][c], up[2][c], up[3][c])
        - recon_rest(down[4][c], down[3][c], down[2][c], down[1][c])
        for c in range(5)
    ]
    outer = t[0] + t[4]
    shared = outer + t[1]
    swing = s * (t[4] - t[0])
    back = [
        shared,
        a * shared + swing,
        b * shared + t[2],
        e * shared + t[3],
        h * outer + k * t[1] + b * t[2] + e * t[3] + a * swing,
    ]
    rest = [None] * 5
    for position, component in enumerate(order):
        rest[component] = (1.0 / 6.0) * (linear[position] - back[position])
    return rest


def along_lanes(any_ref, q_ref, mask_ref, out_ref, d_ref, s_ref, m_ref, g_ref, x_ref):
    normal = 2
    groups = q_ref.shape[3] // LANES

    def parts(value):
        return [value[:, g * LANES : (g + 1) * LANES] for g in range(groups)]

    def prev(value):
        return pltpu.roll(value, 1, 1)

    def put(ref, index, value):
        for g, part in enumerate(parts(value)):
            ref[(g,) + index] = part

    width = q_ref.shape[3]

    def tile(row, carry):
        rows = pl.ds(pl.multiple_of(row * ROWS, ROWS), ROWS)
        q = [q_ref[c, 0, rows, :] for c in range(5)]
        half_vel, half_enth, pressure, total, sound = cell_values(q[0], q[1:4], q[4])
        flux = half_flux(q[1:4], half_vel, pressure, total, normal)
        wave = jnp.abs(2.0 * half_vel[normal]) + sound
        for position, n in enumerate(pair_order(normal)):
            put(m_ref, (position,), half_vel[n] + prev(half_vel[n]))
        put(m_ref, (3,), half_enth + prev(half_enth))
        two = jnp.maximum(wave, prev(wave))
        alpha = jnp.maximum(jnp.maximum(pltpu.roll(two, 2, 1), two), pltpu.roll(two, width - 2, 1))
        put(m_ref, (4,), alpha)
        for c in range(5):
            before = prev(flux[c])
            put(s_ref, (c,), flux[c] + before)
            diff = flux[c] - before
            half = 0.5 * q[c]
            diff_q = half - prev(half)
            for step, amount in enumerate((2, 1, 0, width - 1, width - 2)):
                put(d_ref, (step, c), pltpu.roll(diff, amount, 1) if amount else diff)
                put(d_ref, (step, 5 + c), pltpu.roll(diff_q, amount, 1) if amount else diff_q)

        def face(g, carry):
            d_flux = [[d_ref[g, k, c] for c in range(5)] for k in range(5)]
            rest = central_rest(d_flux)
            for c in range(5):
                g_ref[g, c] = s_ref[g, c] + rest[c]

            @pl.when(any_ref[g] > 0)
            def _():
                d_flux = [[d_ref[g, k, c] for c in range(5)] for k in range(5)]
                d_state = [[d_ref[g, k, 5 + c] for c in range(5)] for k in range(5)]
                rest = central_rest(d_flux)
                mean = [m_ref[g, n] for n in range(4)]
                weno = weno_rest(d_flux, d_state, mean, m_ref[g, 4], normal)
                for c in range(5):
                    x_ref[g, c] = weno[c] - rest[c]

            @pl.when(any_ref[g] <= 0)
            def _():
                for c in range(5):
                    x_ref[g, c] = jnp.zeros((ROWS, LANES), jnp.float32)

            return carry

        lax.fori_loop(0, groups, face, 0)
        shock = mask_ref[...] > 0.0
        for c in range(5):
            full = jnp.concatenate([g_ref[g, c] for g in range(groups)], axis=1)
            more = jnp.concatenate([x_ref[g, c] for g in range(groups)], axis=1)
            base = full - pltpu.roll(full, width - 1, 1)
            extra = more - pltpu.roll(more, width - 1, 1)
            out_ref[c, 0, rows, :] = base + jnp.where(shock, extra, 0.0)
        return carry

    lax.fori_loop(0, q_ref.shape[2] // ROWS, tile, 0)


def along_others(
    any_ref, step_ref, q_ref, xl_ref, xr_ref, yl_ref, yr_ref, az_ref, mask_ref, adv_ref, ten_ref, p_ref, ty_ref
):
    group = pl.program_id(0)
    size_x, size_y = q_ref.shape[1], q_ref.shape[2]
    q_flat = q_ref.reshape(5, size_x * size_y, LANES)
    ty_flat = ty_ref.reshape(5, size_y * size_x, LANES)
    shock = mask_ref[...] > 0.0

    def cells(start, count, load, carry, normal):
        def body(i, before):
            q = load(i)
            half_vel, half_enth, pressure, total, sound = cell_values(q[0], q[1:4], q[4])
            flux = half_flux(q[1:4], half_vel, pressure, total, normal)
            wave = jnp.abs(2.0 * half_vel[normal]) + sound
            half = [0.5 * v for v in q]
            vel = [half_vel[n] for n in pair_order(normal)] + [half_enth]
            now = flux + half + vel + [wave]
            at = start + i
            for c in range(10):
                p_ref[at, c] = now[c] - before[c]
            for c in range(5):
                p_ref[at, 10 + c] = now[c] + before[c]
            for c in range(4):
                p_ref[at, 15 + c] = now[10 + c] + before[10 + c]
            p_ref[at, 19] = jnp.maximum(now[14], before[14])
            return tuple(now)

        return lax.fori_loop(0, count, body, carry)

    def faces(normal, store, with_weno):
        def body(j, before):
            d_flux = [[p_ref[j - 2 + k, c] for c in range(5)] for k in range(5)]
            rest = central_rest(d_flux)
            now = [p_ref[j, 10 + c] + rest[c] for c in range(5)]
            if with_weno:
                d_state = [[p_ref[j - 2 + k, 5 + c] for c in range(5)] for k in range(5)]
                mean = [p_ref[j, 15 + n] for n in range(4)]
                alpha = jnp.maximum(jnp.maximum(p_ref[j - 2, 19], p_ref[j, 19]), p_ref[j + 2, 19])
                weno = weno_rest(d_flux, d_state, mean, alpha, normal)
                now = now + [weno[c] - rest[c] for c in range(5)]
            at = jnp.maximum(j - 4, 0)
            for c in range(5):
                diff = before[c] - now[c]
                if with_weno:
                    diff = diff + jnp.where(shock, before[5 + c] - now[5 + c], 0.0)
                store(at, c, diff)
            return tuple(now)

        zero = jnp.zeros((ROWS, LANES), jnp.float32)
        count = 10 if with_weno else 5
        lax.fori_loop(3, 4 + size_x, body, (zero,) * count)

    def line(normal, left, middle, right, store):
        zero = jnp.zeros((ROWS, LANES), jnp.float32)
        carry = (zero,) * 15
        carry = cells(0, 3, left, carry, normal)
        carry = cells(3, size_x, middle, carry, normal)
        cells(3 + size_x, 3, right, carry, normal)

        @pl.when(any_ref[4 + group] > 0)
        def _():
            faces(normal, store, True)

        @pl.when(any_ref[4 + group] <= 0)
        def _():
            faces(normal, store, False)

    def line_x(t, carry):
        rows = pl.ds(pl.multiple_of(t * ROWS, ROWS), ROWS)

        def store(at, c, diff):
            ten_ref[c, at, rows, :] = az_ref[c, at, rows, :] + diff

        line(
            0,
            lambda i: [xl_ref[c, i, rows, :] for c in range(5)],
            lambda i: [q_ref[c, i, rows, :] for c in range(5)],
            lambda i: [xr_ref[c, i, rows, :] for c in range(5)],
            store,
        )
        return carry

    def line_y(t, carry):
        rows = pl.ds(pl.multiple_of(t * ROWS, ROWS), ROWS)

        def store(at, c, diff):
            ty_ref[c, at, rows, :] = diff

        line(
            1,
            lambda i: [yl_ref[c, i, rows, :] for c in range(5)],
            lambda i: [q_flat[c, pl.ds(t * (ROWS * size_y) + i, ROWS, stride=size_y), :] for c in range(5)],
            lambda i: [yr_ref[c, i, rows, :] for c in range(5)],
            store,
        )
        return carry

    lax.fori_loop(0, size_y // ROWS, line_x, 0)
    lax.fori_loop(0, size_x // ROWS, line_y, 0)
    step = step_ref[0]

    def last(x, carry):
        for t in range(size_y // ROWS):
            rows = pl.ds(t * ROWS, ROWS)
            for c in range(5):
                other = ty_flat[c, pl.ds(t * (ROWS * size_x) + x, ROWS, stride=size_x), :]
                total = ten_ref[c, x, rows, :] + other
                ten_ref[c, x, rows, :] = total
                adv_ref[c, x, rows, :] = q_ref[c, x, rows, :] + step * total
        return carry

    lax.fori_loop(0, size_x, last, 0)


def call_lanes(needs, conserved, mask):
    _, size_x, size_y, size_z = conserved.shape
    groups = size_z // LANES
    tile = (ROWS, LANES)
    return pl.pallas_call(
        along_lanes,
        out_shape=jax.ShapeDtypeStruct(conserved.shape, jnp.float32),
        grid=(size_x,),
        in_specs=[
            pl.BlockSpec(memory_space=pltpu.SMEM),
            pl.BlockSpec((5, 1, size_y, size_z), lambda x: (0, x, 0, 0)),
            pl.BlockSpec((1, size_z), lambda x: (0, 0)),
        ],
        out_specs=pl.BlockSpec((5, 1, size_y, size_z), lambda x: (0, x, 0, 0)),
        scratch_shapes=[
            pltpu.VMEM((groups, 5, 10) + tile, jnp.float32),
            pltpu.VMEM((groups, 5) + tile, jnp.float32),
            pltpu.VMEM((groups, 5) + tile, jnp.float32),
            pltpu.VMEM((groups, 5) + tile, jnp.float32),
            pltpu.VMEM((groups, 5) + tile, jnp.float32),
        ],
        cost_estimate=pl.CostEstimate(flops=120_000_000, bytes_accessed=2 * conserved.size * 4, transcendentals=0),
        name="along_lanes",
    )(needs, conserved, mask)


def call_others(needs, step, conserved, x_low, x_high, y_low, y_high, part, mask):
    _, size_x, size_y, size_z = conserved.shape
    groups = size_z // LANES
    tile = (ROWS, LANES)

    def spec(first, second):
        return pl.BlockSpec((5, first, second, LANES), lambda g: (0, 0, 0, g))

    smem = pl.BlockSpec(memory_space=pltpu.SMEM)
    whole = spec(size_x, size_y)
    return pl.pallas_call(
        along_others,
        out_shape=[jax.ShapeDtypeStruct(conserved.shape, jnp.float32)] * 2,
        grid=(groups,),
        in_specs=[
            smem,
            smem,
            whole,
            spec(3, size_y),
            spec(3, size_y),
            spec(3, size_x),
            spec(3, size_x),
            whole,
            pl.BlockSpec((1, LANES), lambda g: (0, g)),
        ],
        out_specs=[whole, whole],
        scratch_shapes=[
            pltpu.VMEM((size_x + 6, 20) + tile, jnp.float32),
            pltpu.VMEM((5, size_y, size_x, LANES), jnp.float32),
        ],
        cost_estimate=pl.CostEstimate(flops=240_000_000, bytes_accessed=4 * conserved.size * 4, transcendentals=0),
        name="along_others",
    )(needs, step, conserved, x_low, x_high, y_low, y_high, part, mask)


def speed_max(fields):
    density = fields[0]
    kinetic = 0.5 * (fields[1] * fields[1] + fields[2] * fields[2] + fields[3] * fields[3])
    pressure = GAMMA_LESS * (fields[4] - kinetic / density)
    sound_speed = jnp.sqrt(GAMMA * pressure / density)
    total = jnp.abs(fields[1]) + jnp.abs(fields[2]) + jnp.abs(fields[3])
    return jnp.max(total / density + 3.0 * sound_speed)


def needs_of(flags, groups):
    per = flags.shape[0] // groups
    own = jnp.max(flags.reshape(groups, per), axis=1)
    last = jnp.roll(flags.reshape(groups, per)[:, -1], 1)
    return jnp.concatenate([jnp.maximum(own, last), own])


def pieces(axis, shard, dim):
    size = lax.axis_size(axis)
    length = shard.shape[dim]
    up = [(i, (i + 1) % size) for i in range(size)]
    down = [(j, i) for i, j in up]
    last = lax.slice_in_dim(shard, length - 3, length, axis=dim)
    first = lax.slice_in_dim(shard, 0, 3, axis=dim)
    if dim == 2:
        last, first = (jnp.swapaxes(v, 1, 2) for v in (last, first))
    return lax.ppermute(last, axis, up), lax.ppermute(first, axis, down)


def top_of_all(value):
    count = lax.axis_size("gx") * lax.axis_size("gy")
    rows = jnp.full((count, LANES), value, jnp.float32)
    return jnp.max(lax.all_to_all(rows, ("gx", "gy"), 0, 0, tiled=True))


def shards(conserved, shock_flags):
    size_x, size_z = conserved.shape[1], conserved.shape[3]
    flags = shock_flags[0, 0]
    top = speed_max(conserved)
    x_low, x_high = pieces("gx", conserved, 1)
    y_low, y_high = pieces("gy", conserved, 2)
    step = (COURANT / top_of_all(top)).reshape(1)
    mask = jnp.repeat(flags, size_x).astype(jnp.float32)[None, :]
    needs = needs_of(flags, size_z // LANES)
    part = call_lanes(needs, conserved, mask)
    advanced, tendency = call_others(needs, step, conserved, x_low, x_high, y_low, y_high, part, mask)
    return advanced, tendency


def solution(mesh):
    return jax.shard_map(
        shards,
        mesh=mesh,
        in_specs=(P(None, "gx", "gy", None), P("gx", "gy", None)),
        out_specs=(P(None, "gx", "gy", None), P(None, "gx", "gy", None)),
        check_vma=False,
    )
```

```python
import functools

import jax
import jax.numpy as jnp
from jax import lax
from jax.experimental import pallas as pl
from jax.experimental.pallas import tpu as pltpu
from jax.sharding import PartitionSpec as P

GAMMA = 1.4
GAMMA_LESS = 0.4
COURANT = 0.4
EPSILON = 1e-06
LANES = 128
ROWS = 8
TINY = 1e-37


def cell_values(density, mom, energy, normal):
    inv = 1.0 / density
    inv_half = 0.5 * inv
    half_vel = [m * inv_half for m in mom]
    kinetic = mom[0] * half_vel[0] + mom[1] * half_vel[1] + mom[2] * half_vel[2]
    pressure = GAMMA_LESS * (energy - kinetic)
    total = energy + pressure
    sound_sq = GAMMA * pressure * inv
    sound = sound_sq * lax.rsqrt(jnp.maximum(sound_sq, TINY))
    half = [0.5 * v for v in (density, *mom, energy)]
    half_normal = half_vel[normal]
    flux = [half[1 + normal]]
    for other in range(3):
        part = mom[other] * half_normal
        flux.append(part + 0.5 * pressure if other == normal else part)
    flux.append(total * half_normal)
    means = [half_vel[n] for n in pair_order(normal)] + [total * inv_half]
    return half, flux, means, jnp.abs(2.0 * half_normal) + sound


def pair_order(normal):
    return [normal] + [other for other in range(3) if other != normal]


def recon_rest(d1, d2, d3, d4):
    t1 = d2 - d1
    t2 = d3 - d2
    t3 = d4 - d3
    d2s = 0.75 * d2
    d3s = 0.75 * d3
    p2 = d2s * d2 + 0.75 * EPSILON
    p3 = d3s * d3 + 0.75 * EPSILON
    r0 = 1.0 / (t1 * (t1 + d2s) + p2)
    r1 = 1.0 / (t2 * (t2 + d2s) + p2)
    r2 = 1.0 / (t3 * (t3 - d3s) + p3)
    z0 = r0 * r0
    z1 = r1 * r1
    z2 = 1.5 * (r2 * r2)
    num = z0 * (t2 - t1) + z2 * (t3 - t2)
    den = z2 + (0.5 * z0 + 3.0 * z1)
    return num * (1.0 / den)


def central_face(sums, d_flux):
    return [
        sums[c] + (1.0 / 30.0) * ((d_flux[4][c] - d_flux[0][c]) - 7.0 * (d_flux[3][c] - d_flux[1][c]))
        for c in range(5)
    ]


def face_terms(means):
    a, b, e, h = means
    k = 0.5 * (a * a + b * b + e * e)
    s_sq = GAMMA_LESS * (h - k)
    inv_s = lax.rsqrt(s_sq)
    return [a, b, e, h, k, s_sq * inv_s, (0.5 * GAMMA_LESS) * (inv_s * inv_s), 0.5 * inv_s]


def face_order(normal):
    return [0] + [1 + n for n in pair_order(normal)] + [4]


def weno_waves(d_flux, d_state, terms, alpha, normal):
    order = face_order(normal)
    a, b, e, _, k, _, half_g, half_inv = terms

    def project(x):
        x1 = x[1] - a * x[0]
        x2 = x[2] - b * x[0]
        x3 = x[3] - e * x[0]
        y = half_g * (x[4] - a * x1 - b * x2 - e * x3 - k * x[0])
        z = half_inv * x1
        return [y - z, x[0] - (y + y), x2, x3, y + z]

    up = []
    down = []
    for step in range(5):
        scaled = [alpha * d_state[step][c] for c in order]
        flux = [d_flux[step][c] for c in order]
        up.append([f + q for f, q in zip(flux, scaled)] if step < 4 else None)
        down.append([f - q for f, q in zip(flux, scaled)] if step > 0 else None)
    linear = [(up[1][c] - down[3][c]) - (up[2][c] - down[2][c]) for c in range(5)]
    up = [project(x) if x is not None else None for x in up]
    down = [project(x) if x is not None else None for x in down]
    waves = [
        recon_rest(up[0][c], up[1][c], up[2][c], up[3][c])
        - recon_rest(down[4][c], down[3][c], down[2][c], down[1][c])
        for c in range(5)
    ]
    return linear, waves


def weno_face(sums, linear, waves, terms, normal):
    a, b, e, h, k, s = terms[:6]
    outer = waves[0] + waves[4]
    shared = outer + waves[1]
    swing = s * (waves[4] - waves[0])
    back = [
        shared,
        a * shared + swing,
        b * shared + waves[2],
        e * shared + waves[3],
        h * outer + k * waves[1] + b * waves[2] + e * waves[3] + a * swing,
    ]
    face = [None] * 5
    for position, component in enumerate(face_order(normal)):
        face[component] = sums[component] + (1.0 / 6.0) * (linear[position] - back[position])
    return face


class Line:
    def __init__(self, refs, normal, unit):
        self.v_ref, self.p_ref, self.w_ref, self.f_ref = refs
        self.normal = normal
        self.unit = unit

    def rows(self, i, off=0):
        start = i * ROWS + off * self.unit
        if (off * self.unit) % ROWS == 0 and not isinstance(i, int):
            start = pl.multiple_of(start, ROWS)
        return pl.ds(start, ROWS)

    def cell(self, i, q):
        n = self.normal
        half, flux, means, wave = cell_values(q[0], q[1:4], q[4], n)
        now = half + flux[1:] + means + [wave]
        here, prev = self.rows(i), self.rows(i, -1)
        for v in range(14):
            self.v_ref[v, here, :] = now[v]
        before = [self.v_ref[v, prev, :] for v in range(14)]
        for v in range(9):
            self.p_ref[v, here, :] = now[v] - before[v]
        self.p_ref[9, here, :] = now[1 + n] + before[1 + n]
        for v in range(5, 9):
            self.p_ref[5 + v, here, :] = now[v] + before[v]
        self.p_ref[14, here, :] = jnp.maximum(now[13], before[13])
        terms = face_terms([now[v] + before[v] for v in range(9, 13)])
        for v in range(8):
            self.p_ref[15 + v, here, :] = terms[v]

    def pair(self, v, j, off=0):
        return self.p_ref[v, self.rows(j, off), :]

    def fluxes(self, j):
        return [[self.pair(4 + c if c else 1 + self.normal, j, k - 2) for c in range(5)] for k in range(5)]

    def central(self, j, d_flux):
        face = central_face([self.pair(9 + c, j) for c in range(5)], d_flux)
        for c in range(5):
            self.f_ref[c, self.rows(j), :] = face[c]

    def waves(self, j, d_flux):
        d_state = [[self.pair(c, j, k - 2) for c in range(5)] for k in range(5)]
        terms = [self.pair(15 + v, j) for v in range(8)]
        alpha = jnp.maximum(jnp.maximum(self.pair(14, j, -2), self.pair(14, j)), self.pair(14, j, 2))
        linear, waves = weno_waves(d_flux, d_state, terms, alpha, self.normal)
        for c in range(5):
            self.w_ref[c, self.rows(j), :] = linear[c]
            self.w_ref[5 + c, self.rows(j), :] = waves[c]

    def face(self, j):
        both = [self.w_ref[c, self.rows(j), :] for c in range(10)]
        terms = [self.pair(15 + v, j) for v in range(6)]
        face = weno_face([self.pair(9 + c, j) for c in range(5)], both[:5], both[5:], terms, self.normal)
        for c in range(5):
            self.f_ref[5 + c, self.rows(j), :] = face[c]

    def change(self, j, first):
        here, following = self.rows(j), self.rows(j, 1)
        return [self.f_ref[first + c, here, :] - self.f_ref[first + c, following, :] for c in range(5)]


def along_lanes(flag_ref, q_ref, out_ref, z_ref, v_ref, p_ref, w_ref, f_ref):
    size_x, size_y, width = q_ref.shape[1:]
    lines = size_x * size_y
    q_flat = q_ref.reshape(5, lines, width)
    out_flat = out_ref.reshape(5, lines, width)
    groups = width // LANES
    steps = width // ROWS
    blocks = flag_ref.shape[2]
    per_block = steps // blocks
    line = Line((v_ref, p_ref, w_ref, f_ref), 2, 1)

    def turn_in(g, carry):
        lanes = pl.ds(pl.multiple_of(g * LANES, LANES), LANES)
        for c in range(5):
            z_ref[c, lanes, :] = q_flat[c, :, lanes].T
        return carry

    def turn_out(g, carry):
        lanes = pl.ds(pl.multiple_of(g * LANES, LANES), LANES)
        for c in range(5):
            out_flat[c, :, lanes] = z_ref[5 + c, lanes, :].T
        return carry

    def chunk_of(i):
        return lax.rem(jnp.int32(i + (steps - 2)), steps)

    def fetch(i):
        at = chunk_of(i)
        rows = pl.ds(pl.multiple_of(at * ROWS, ROWS), ROWS)
        return [z_ref[c, rows, :] for c in range(5)]

    def block_of(i):
        return chunk_of(i) // per_block

    def finish(j):
        at = jnp.maximum(j - 2, 0)
        rows = pl.ds(pl.multiple_of(at * ROWS, ROWS), ROWS)
        first = jnp.where(flag_ref[0, 0, block_of(j)] > 0, 5, 0)
        for c, value in enumerate(line.change(j, first)):
            z_ref[5 + c, rows, :] = value

    lax.fori_loop(0, groups, turn_in, 0)

    def lead(i, carry):
        line.cell(i, fetch(i))
        return carry

    lax.fori_loop(1, 4, lead, 0)

    def needed(i):
        return flag_ref[0, 0, block_of(i)] + flag_ref[0, 0, block_of(i - 1)]

    def body(i, carry):
        sharp = needed(i) + needed(i - 1)

        @pl.when(sharp > 0)
        def _():
            line.face(i - 1)
            finish(i - 2)
            d_flux = line.fluxes(i)
            line.waves(i, d_flux)
            line.central(i, d_flux)
            line.cell(i + 2, fetch(i + 2))

        @pl.when(sharp <= 0)
        def _():
            finish(i - 2)
            line.central(i, line.fluxes(i))
            line.cell(i + 2, fetch(i + 2))

        return carry

    lax.fori_loop(2, steps + 2, body, 0)
    line.face(steps + 1)
    for c in range(10):
        f_ref[c, pl.ds(ROWS * (steps + 2), ROWS), :] = f_ref[c, pl.ds(2 * ROWS, ROWS), :]
    finish(steps)
    finish(steps + 1)
    lax.fori_loop(0, groups, turn_out, 0)


def along_others(
    flag_ref, top_ref, q_ref, xl_ref, xr_ref, yl_ref, yr_ref, za_ref, zb_ref, adv_ref, ten_ref, v_ref, p_ref, w_ref, f_ref, ty_ref
):
    group = pl.program_id(0)
    size_x, size_y = q_ref.shape[1], q_ref.shape[2]
    q_flat = q_ref.reshape(5, size_x * size_y, LANES)
    ty_flat = ty_ref.reshape(5, size_y * size_x, LANES)
    per_group = flag_ref.shape[2] // pl.num_programs(0)
    edge = LANES // per_group
    lane_block = lax.broadcasted_iota(jnp.int32, (ROWS, LANES), 1) // edge
    marks = jnp.zeros((ROWS, LANES), jnp.int32)
    some = jnp.int32(0)
    for b in range(per_group):
        flag = flag_ref[0, 0, group * per_group + b]
        marks = jnp.where(lane_block == b, flag, marks)
        some = jnp.maximum(some, flag)
    shock = marks > 0

    def march(normal, count, left, middle, right, store):
        line = Line((v_ref, p_ref, w_ref, f_ref), normal, ROWS)

        def from_left(i, carry):
            line.cell(1 + i, left(i))
            return carry

        def from_middle(i, carry):
            line.cell(4 + i, middle(i))
            return carry

        lax.fori_loop(0, 3, from_left, 0)
        lax.fori_loop(0, 3, from_middle, 0)

        def ahead(j):
            inner = j - 1 < count
            near = middle(jnp.minimum(j - 1, count - 1))
            far = right(jnp.clip(j - 1 - count, 0, 2))
            line.cell(j + 3, [jnp.where(inner, n, f) for n, f in zip(near, far)])

        def finish(j, sharp):
            at = jnp.maximum(j - 4, 0)
            change = line.change(j, 0)
            if sharp:
                change = [jnp.where(shock, w, c) for w, c in zip(line.change(j, 5), change)]
            for c in range(5):
                store(at, c, change[c])

        @pl.when(some > 0)
        def _():
            def body(j, carry):
                line.face(j - 1)
                finish(j - 2, True)
                d_flux = line.fluxes(j)
                line.waves(j, d_flux)
                line.central(j, d_flux)
                ahead(j)
                return carry

            lax.fori_loop(4, 5 + count, body, 0)
            line.face(4 + count)
            finish(3 + count, True)

        @pl.when(some <= 0)
        def _():
            def body(j, carry):
                ahead(j)
                line.central(j, line.fluxes(j))
                finish(j - 1, False)
                return carry

            lax.fori_loop(4, 5 + count, body, 0)

    def line_x(t, carry):
        rows = pl.ds(pl.multiple_of(t * ROWS, ROWS), ROWS)

        def store(at, c, value):
            ten_ref[c, at, rows, :] = value

        march(
            0,
            size_x,
            lambda i: [xl_ref[c, i, rows, :] for c in range(5)],
            lambda i: [q_ref[c, i, rows, :] for c in range(5)],
            lambda i: [xr_ref[c, i, rows, :] for c in range(5)],
            store,
        )
        return carry

    def line_y(t, carry):
        rows = pl.ds(pl.multiple_of(t * ROWS, ROWS), ROWS)

        def store(at, c, value):
            ty_ref[c, at, rows, :] = value

        march(
            1,
            size_y,
            lambda i: [yl_ref[c, i, rows, :] for c in range(5)],
            lambda i: [q_flat[c, pl.ds(t * (ROWS * size_y) + i, ROWS, stride=size_y), :] for c in range(5)],
            lambda i: [yr_ref[c, i, rows, :] for c in range(5)],
            store,
        )
        return carry

    lax.fori_loop(0, size_y // ROWS, line_x, 0)
    lax.fori_loop(0, size_x // ROWS, line_y, 0)
    step = COURANT / jnp.max(top_ref[...], axis=0, keepdims=True)
    half = size_x // 2

    def last(x, carry):
        for h, part_ref in enumerate((za_ref, zb_ref)):
            for t in range(size_y // ROWS):
                rows = pl.ds(t * ROWS, ROWS)
                for c in range(5):
                    at = h * half + x
                    other = ty_flat[c, pl.ds(t * (ROWS * size_x) + at, ROWS, stride=size_x), :]
                    total = ten_ref[c, at, rows, :] + other + part_ref[c, x, rows, :]
                    ten_ref[c, at, rows, :] = total
                    adv_ref[c, at, rows, :] = q_ref[c, at, rows, :] + step * total
        return carry

    lax.fori_loop(0, half, last, 0)


def prepare(q_ref, xf_ref, xl_ref, yf_ref, yl_ref, top_ref, acc_ref):
    size_x, size_y = q_ref.shape[1], q_ref.shape[2]
    q_flat = q_ref.reshape(5, size_x * size_y, LANES)
    group = pl.program_id(0)

    @pl.when(group == 0)
    def _():
        acc_ref[...] = jnp.zeros_like(acc_ref)

    def speeds(x, top):
        for t in range(size_y // ROWS):
            q = [q_ref[c, x, pl.ds(t * ROWS, ROWS), :] for c in range(5)]
            inv = 1.0 / q[0]
            kinetic = 0.5 * (q[1] * q[1] + q[2] * q[2] + q[3] * q[3]) * inv
            sound_sq = (GAMMA * GAMMA_LESS) * (q[4] - kinetic) * inv
            sound = sound_sq * lax.rsqrt(jnp.maximum(sound_sq, TINY))
            total = (jnp.abs(q[1]) + jnp.abs(q[2]) + jnp.abs(q[3])) * inv + 3.0 * sound
            top = jnp.maximum(top, total)
        return top

    acc_ref[...] = lax.fori_loop(0, size_x, speeds, acc_ref[...])
    for c in range(5):
        for k in range(3):
            xf_ref[c, k] = q_ref[c, k]
            xl_ref[c, k] = q_ref[c, size_x - 3 + k]
            for t in range(size_x // ROWS):
                rows = pl.ds(t * ROWS, ROWS)
                first = t * ROWS * size_y
                yf_ref[c, k, rows, :] = q_flat[c, pl.ds(first + k, ROWS, stride=size_y), :]
                yl_ref[c, k, rows, :] = q_flat[c, pl.ds(first + size_y - 3 + k, ROWS, stride=size_y), :]

    @pl.when(group == pl.num_programs(0) - 1)
    def _():
        top_ref[...] = jnp.full(top_ref.shape, jnp.max(acc_ref[...]), jnp.float32)


def line_scratch(rows):
    return [pltpu.VMEM((count, rows, LANES), jnp.float32) for count in (14, 23, 10, 10)]


def call_prepare(conserved, rows):
    _, size_x, size_y, size_z = conserved.shape

    def spec(first, second):
        return pl.BlockSpec((5, first, second, LANES), lambda g: (0, 0, 0, g))

    layers = jax.ShapeDtypeStruct((5, 3, size_y, size_z), jnp.float32)
    turned = jax.ShapeDtypeStruct((5, 3, size_x, size_z), jnp.float32)
    return pl.pallas_call(
        prepare,
        out_shape=[layers, layers, turned, turned, jax.ShapeDtypeStruct((rows, LANES), jnp.float32)],
        grid=(size_z // LANES,),
        in_specs=[spec(size_x, size_y)],
        out_specs=[spec(3, size_y), spec(3, size_y), spec(3, size_x), spec(3, size_x)]
        + [pl.BlockSpec((rows, LANES), lambda g: (0, 0))],
        scratch_shapes=[pltpu.VMEM((ROWS, LANES), jnp.float32)],
        cost_estimate=pl.CostEstimate(flops=4_000_000, bytes_accessed=2 * conserved.size * 4, transcendentals=0),
        name="prepare",
    )(conserved)


def call_lanes(flags, conserved, part):
    _, size_x, size_y, size_z = conserved.shape
    chunk = LANES // size_y
    block = (5, chunk, size_y, size_z)
    return pl.pallas_call(
        along_lanes,
        out_shape=jax.ShapeDtypeStruct(block, jnp.float32),
        grid=(1,),
        in_specs=[pl.BlockSpec(memory_space=pltpu.SMEM), pl.BlockSpec(block, lambda _: (0, part, 0, 0))],
        out_specs=pl.BlockSpec(block, lambda _: (0, 0, 0, 0)),
        scratch_shapes=[pltpu.VMEM((10, size_z, LANES), jnp.float32)] + line_scratch(size_z + 5 * ROWS),
        cost_estimate=pl.CostEstimate(flops=60_000_000, bytes_accessed=conserved.size * 4, transcendentals=0),
        name="along_lanes",
    )(flags, conserved)


def call_others(flags, top, conserved, x_low, x_high, y_low, y_high, parts):
    _, size_x, size_y, size_z = conserved.shape

    def spec(first, second):
        return pl.BlockSpec((5, first, second, LANES), lambda g: (0, 0, 0, g))

    whole = spec(size_x, size_y)
    return pl.pallas_call(
        along_others,
        out_shape=[jax.ShapeDtypeStruct(conserved.shape, jnp.float32)] * 2,
        grid=(size_z // LANES,),
        in_specs=[
            pl.BlockSpec(memory_space=pltpu.SMEM),
            pl.BlockSpec(top.shape, lambda g: (0, 0)),
            whole,
            spec(3, size_y),
            spec(3, size_y),
            spec(3, size_x),
            spec(3, size_x),
            spec(size_x // 2, size_y),
            spec(size_x // 2, size_y),
        ],
        out_specs=[whole, whole],
        scratch_shapes=line_scratch((max(size_x, size_y) + 9) * ROWS)
        + [pltpu.VMEM((5, size_y, size_x, LANES), jnp.float32)],
        cost_estimate=pl.CostEstimate(flops=240_000_000, bytes_accessed=4 * conserved.size * 4, transcendentals=0),
        name="along_others",
    )(flags, top, conserved, x_low, x_high, y_low, y_high, *parts)


GX = ("ga", "gb")
SPLIT = 4


def neighbours(axis, first, last):
    size = lax.axis_size(axis)
    up = [(i, (i + 1) % size) for i in range(size)]
    down = [(j, i) for i, j in up]
    return lax.ppermute(last, axis, up), lax.ppermute(first, axis, down)


def swap(rows, axes):
    return lax.all_to_all(rows, axes, 0, 0, tiled=True)


def shards(conserved, shock_flags):
    inner, outer = ("gb",), ("ga", "gy")
    count, others = lax.axis_size(inner), lax.axis_size(outer)
    x_first, x_last, y_first, y_last, top = call_prepare(conserved, count)
    x_low, x_high = neighbours(GX, x_first, x_last)
    y_low, y_high = neighbours("gy", y_first, y_last)
    top = swap(top, inner)
    parts = [call_lanes(shock_flags, conserved, 0)]
    top, parts[0] = lax.optimization_barrier((top, parts[0]))
    top = swap(jnp.broadcast_to(jnp.max(top, axis=0, keepdims=True), (others, LANES)), outer)
    parts.append(call_lanes(shock_flags, conserved, 1))
    return call_others(shock_flags, top, conserved, x_low, x_high, y_low, y_high, parts)


def local(conserved, shock_flags, top, x_low, x_high, y_low, y_high):
    x_first, x_last, y_first, y_last, mine = call_prepare(conserved, 16)
    parts = [call_lanes(shock_flags, conserved, h) for h in range(2)]
    return call_others(shock_flags, mine, conserved, x_last, x_first, y_last, y_first, parts)


def solution(mesh):
    devices = mesh.devices
    size_x, size_y = devices.shape
    mesh = jax.sharding.Mesh(devices.reshape(SPLIT, size_x // SPLIT, size_y), (*GX, "gy"))
    spec = P(None, GX, "gy", None)
    return jax.shard_map(
        shards,
        mesh=mesh,
        in_specs=(spec, P(GX, "gy", None)),
        out_specs=(spec, spec),
        check_vma=False,
    )
```

```python
import functools

import jax
import jax.numpy as jnp
from jax import lax
from jax.experimental import pallas as pl
from jax.experimental.pallas import tpu as pltpu
from jax.sharding import PartitionSpec as P

GAMMA = 1.4
GAMMA_LESS = 0.4
COURANT = 0.4
EPSILON = 1e-06
LANES = 128
ROWS = 8
TINY = 1e-37


def cell_values(density, mom, energy, normal):
    inv = 1.0 / density
    inv_half = 0.5 * inv
    half_vel = [m * inv_half for m in mom]
    kinetic = mom[0] * half_vel[0] + mom[1] * half_vel[1] + mom[2] * half_vel[2]
    pressure = GAMMA_LESS * (energy - kinetic)
    total = energy + pressure
    sound_sq = GAMMA * pressure * inv
    sound = sound_sq * lax.rsqrt(jnp.maximum(sound_sq, TINY))
    half_normal = half_vel[normal]
    flux = [0.5 * mom[normal]]
    for other in range(3):
        part = mom[other] * half_normal
        flux.append(part + 0.5 * pressure if other == normal else part)
    flux.append(total * half_normal)
    means = [half_vel[n] for n in pair_order(normal)] + [total * inv_half]
    return flux, means, jnp.abs(half_normal) + 0.5 * sound


def pair_order(normal):
    return [normal] + [other for other in range(3) if other != normal]


def recon_rest(d1, d2, d3, d4):
    t1 = d2 - d1
    t2 = d3 - d2
    t3 = d4 - d3
    d2s = 0.75 * d2
    d3s = 0.75 * d3
    p2 = d2s * d2 + 0.75 * EPSILON
    p3 = d3s * d3 + 0.75 * EPSILON
    r0 = 1.0 / (t1 * (t1 + d2s) + p2)
    r1 = 1.0 / (t2 * (t2 + d2s) + p2)
    r2 = 1.0 / (t3 * (t3 - d3s) + p3)
    z0 = r0 * r0
    z1 = r1 * r1
    z2 = 1.5 * (r2 * r2)
    num = z0 * (t2 - t1) + z2 * (t3 - t2)
    den = z2 + (0.5 * z0 + 3.0 * z1)
    return num * (1.0 / den)


def central_rest(d_flux):
    return [
        (1.0 / 30.0) * ((d_flux[4][c] - d_flux[0][c]) - 7.0 * (d_flux[3][c] - d_flux[1][c]))
        for c in range(5)
    ]


def face_terms(means):
    a, b, e, h = means
    k = 0.5 * (a * a + b * b + e * e)
    s_sq = GAMMA_LESS * (h - k)
    inv_s = lax.rsqrt(s_sq)
    return [a, b, e, h, k, s_sq * inv_s, (0.5 * GAMMA_LESS) * (inv_s * inv_s), 0.5 * inv_s]


def face_order(normal):
    return [0] + [1 + n for n in pair_order(normal)] + [4]


def weno_waves(d_flux, d_state, terms, alpha, normal):
    order = face_order(normal)
    a, b, e, _, k, _, half_g, half_inv = terms

    def project(x):
        x1 = x[1] - a * x[0]
        x2 = x[2] - b * x[0]
        x3 = x[3] - e * x[0]
        y = half_g * (x[4] - a * x1 - b * x2 - e * x3 - k * x[0])
        z = half_inv * x1
        return [y - z, x[0] - (y + y), x2, x3, y + z]

    up = []
    down = []
    for step in range(5):
        scaled = [alpha * d_state[step][c] for c in order]
        flux = [d_flux[step][c] for c in order]
        up.append([f + q for f, q in zip(flux, scaled)] if step < 4 else None)
        down.append([f - q for f, q in zip(flux, scaled)] if step > 0 else None)
    linear = [(up[1][c] - down[3][c]) - (up[2][c] - down[2][c]) for c in range(5)]
    up = [project(x) if x is not None else None for x in up]
    down = [project(x) if x is not None else None for x in down]
    waves = [
        recon_rest(up[0][c], up[1][c], up[2][c], up[3][c])
        - recon_rest(down[4][c], down[3][c], down[2][c], down[1][c])
        for c in range(5)
    ]
    return linear, waves


def weno_rest(linear, waves, terms, normal):
    a, b, e, h, k, s = terms[:6]
    outer = waves[0] + waves[4]
    shared = outer + waves[1]
    swing = s * (waves[4] - waves[0])
    back = [
        shared,
        a * shared + swing,
        b * shared + waves[2],
        e * shared + waves[3],
        h * outer + k * waves[1] + b * waves[2] + e * waves[3] + a * swing,
    ]
    rest = [None] * 5
    for position, component in enumerate(face_order(normal)):
        rest[component] = (1.0 / 6.0) * (linear[position] - back[position])
    return rest


class Line:
    def __init__(self, refs, normal, unit):
        self.v_ref, self.p_ref, self.w_ref, self.f_ref = refs
        self.normal = normal
        self.unit = unit

    def rows(self, i, off=0):
        start = i * ROWS + off * self.unit
        if (off * self.unit) % ROWS == 0 and not isinstance(i, int):
            start = pl.multiple_of(start, ROWS)
        return pl.ds(start, ROWS)

    def cell(self, i, q):
        n = self.normal
        flux, means, wave = cell_values(q[0], q[1:4], q[4], n)
        now = list(q) + flux + means + [wave]
        here, prev = self.rows(i), self.rows(i, -1)
        for v in range(15):
            self.v_ref[v, here, :] = now[v]
        before = [self.v_ref[v, prev, :] for v in range(15)]
        for v in range(10):
            self.p_ref[v, here, :] = now[v] - before[v]
        self.p_ref[10, here, :] = jnp.maximum(now[14], before[14])
        terms = face_terms([now[v] + before[v] for v in range(10, 14)])
        for v in range(8):
            self.p_ref[11 + v, here, :] = terms[v]

    def pair(self, v, j, off=0):
        return self.p_ref[v, self.rows(j, off), :]

    def fluxes(self, j):
        return [[self.pair(5 + c, j, k - 2) for c in range(5)] for k in range(5)]

    def central(self, j, d_flux):
        for c, value in enumerate(central_rest(d_flux)):
            self.f_ref[c, self.rows(j), :] = value

    def waves(self, j, d_flux):
        d_state = [[self.pair(c, j, k - 2) for c in range(5)] for k in range(5)]
        terms = [self.pair(11 + v, j) for v in range(8)]
        alpha = jnp.maximum(jnp.maximum(self.pair(10, j, -2), self.pair(10, j)), self.pair(10, j, 2))
        linear, waves = weno_waves(d_flux, d_state, terms, alpha, self.normal)
        for c in range(5):
            self.w_ref[c, self.rows(j), :] = linear[c]
            self.w_ref[5 + c, self.rows(j), :] = waves[c]

    def face(self, j):
        both = [self.w_ref[c, self.rows(j), :] for c in range(10)]
        terms = [self.pair(11 + v, j) for v in range(6)]
        for c, value in enumerate(weno_rest(both[:5], both[5:], terms, self.normal)):
            self.f_ref[5 + c, self.rows(j), :] = value

    def change(self, j, first):
        here, following = self.rows(j), self.rows(j, 1)
        return [self.f_ref[first + c, here, :] - self.f_ref[first + c, following, :] for c in range(5)]

    def mean_change(self, j, c):
        return self.pair(5 + c, j) + self.pair(5 + c, j, 1)


def along_lanes(flag_ref, q_ref, out_ref, z_ref, v_ref, p_ref, w_ref, f_ref):
    size_x, size_y, width = q_ref.shape[1:]
    lines = size_x * size_y
    q_flat = q_ref.reshape(5, lines, width)
    out_flat = out_ref.reshape(5, lines, width)
    groups = width // LANES
    steps = width // ROWS
    blocks = flag_ref.shape[2]
    per_block = steps // blocks
    assert steps & (steps - 1) == 0 and blocks & (blocks - 1) == 0
    line = Line((v_ref, p_ref, w_ref, f_ref), 2, 1)

    def turn_in(g, carry):
        lanes = pl.ds(pl.multiple_of(g * LANES, LANES), LANES)
        for c in range(5):
            z_ref[c, lanes, :] = q_flat[c, :, lanes].T
        return carry

    def turn_out(g, carry):
        lanes = pl.ds(pl.multiple_of(g * LANES, LANES), LANES)
        for c in range(5):
            out_flat[c, :, lanes] = z_ref[5 + c, lanes, :].T
        return carry

    def chunk_of(i):
        return (i + (steps - 2)) & (steps - 1)

    def fetch(i):
        at = chunk_of(i)
        rows = pl.ds(pl.multiple_of(at * ROWS, ROWS), ROWS)
        return [z_ref[c, rows, :] for c in range(5)]


    def flag_of(block):
        return flag_ref[0, 0, (block + blocks) & (blocks - 1)]

    def finish(j, flag):
        j = jnp.maximum(j, 0)
        at = jnp.maximum(j - 2, 0)
        rows = pl.ds(pl.multiple_of(at * ROWS, ROWS), ROWS)
        first = jnp.where(flag > 0, 5, 0)
        for c, value in enumerate(line.change(j, first)):
            z_ref[5 + c, rows, :] = value - line.mean_change(j, c)

    lax.fori_loop(0, groups, turn_in, 0, unroll=True)

    def lead(i, carry):
        line.cell(i, fetch(i))
        return carry

    lax.fori_loop(1, 3 + per_block, lead, 0)

    def body(block, carry):
        start = 2 + block * per_block
        own, one, two = flag_of(block), flag_of(block - 1), flag_of(block - 2)
        steps_here = [start + k for k in range(per_block)]

        def lagging():
            finish(start - per_block - 1, two)
            for i in steps_here[:-1]:
                finish(i - per_block, one)

        @pl.when(own + one + two > 0)
        def _():
            for i in steps_here:
                line.face(i - per_block)
            lagging()
            d_flux = [line.fluxes(i) for i in steps_here]
            for i, d in zip(steps_here, d_flux):
                line.waves(i, d)
            for i, d in zip(steps_here, d_flux):
                line.central(i, d)
            for i in steps_here:
                line.cell(i + per_block + 1, fetch(i + per_block + 1))

        @pl.when(own + one + two <= 0)
        def _():
            lagging()
            for i in steps_here:
                line.central(i, line.fluxes(i))
            for i in steps_here:
                line.cell(i + per_block + 1, fetch(i + per_block + 1))

        return carry

    lax.fori_loop(0, blocks, body, 0)
    for k in range(per_block):
        line.face(steps + 2 - per_block + k)
    for c in range(10):
        f_ref[c, pl.ds(ROWS * (steps + 2), ROWS), :] = f_ref[c, pl.ds(2 * ROWS, ROWS), :]
    for i in range(steps + 1 - per_block, steps + 2):
        finish(i, flag_of((i - 2) // per_block))
    lax.fori_loop(0, groups, turn_out, 0, unroll=True)


def along_others(
    flag_ref, top_ref, q_ref, xl_ref, xr_ref, yl_ref, yr_ref, za_ref, zb_ref, adv_ref, ten_ref, v_ref, p_ref, w_ref, f_ref, ty_ref
):
    group = pl.program_id(0)
    size_x, size_y = q_ref.shape[1], q_ref.shape[2]
    q_flat = q_ref.reshape(5, size_x * size_y, LANES)
    ty_flat = ty_ref.reshape(5, size_y * size_x, LANES)
    per_group = flag_ref.shape[2] // pl.num_programs(0)
    edge = LANES // per_group
    lane_block = lax.broadcasted_iota(jnp.int32, (ROWS, LANES), 1) // edge
    marks = jnp.zeros((ROWS, LANES), jnp.int32)
    some = jnp.int32(0)
    for b in range(per_group):
        flag = flag_ref[0, 0, group * per_group + b]
        marks = jnp.where(lane_block == b, flag, marks)
        some = jnp.maximum(some, flag)
    shock = marks > 0

    def march(normal, count, left, middle, right, store):
        line = Line((v_ref, p_ref, w_ref, f_ref), normal, ROWS)

        def from_left(i, carry):
            line.cell(1 + i, left(i))
            return carry

        def from_middle(i, carry):
            line.cell(4 + i, middle(i))
            return carry

        lax.fori_loop(0, 3, from_left, 0, unroll=True)
        lax.fori_loop(0, 4, from_middle, 0, unroll=True)

        def ahead(j):
            inner = j - 1 < count
            near = middle(jnp.minimum(j - 1, count - 1))
            far = right(jnp.clip(j - 1 - count, 0, 2))
            line.cell(j + 3, [jnp.where(inner, n, f) for n, f in zip(near, far)])

        def finish(j, sharp):
            at = jnp.maximum(j - 4, 0)
            change = line.change(j, 0)
            if sharp:
                change = [jnp.where(shock, w, c) for w, c in zip(line.change(j, 5), change)]
            for c in range(5):
                store(at, c, change[c] - line.mean_change(j, c))

        @pl.when(some > 0)
        def _():
            def waves(steps):
                d_flux = [line.fluxes(j) for j in steps]
                for j, d in zip(steps, d_flux):
                    line.waves(j, d)
                for j, d in zip(steps, d_flux):
                    line.central(j, d)

            def two(n, carry):
                j = 4 + 2 * n
                for k in (2, 1):
                    line.face(j - k)
                for k in (3, 2):
                    finish(j - k, True)
                waves([j, j + 1])
                for k in (1, 2):
                    ahead(j + k)
                return carry

            pairs = (count + 1) // 2
            lax.fori_loop(0, pairs, two, 0)
            left_over = list(range(4 + 2 * pairs, 5 + count))
            waves(left_over)
            for j in [2 + 2 * pairs, 3 + 2 * pairs] + left_over:
                line.face(j)
            for j in range(1 + 2 * pairs, 4 + count):
                finish(j, True)

        @pl.when(some <= 0)
        def _():
            def body(j, carry):
                ahead(j)
                line.central(j, line.fluxes(j))
                finish(j - 1, False)
                return carry

            lax.fori_loop(4, 5 + count, body, 0)

    def line_x(t, carry):
        rows = pl.ds(pl.multiple_of(t * ROWS, ROWS), ROWS)

        def store(at, c, value):
            ten_ref[c, at, rows, :] = value

        march(
            0,
            size_x,
            lambda i: [xl_ref[c, i, rows, :] for c in range(5)],
            lambda i: [q_ref[c, i, rows, :] for c in range(5)],
            lambda i: [xr_ref[c, i, rows, :] for c in range(5)],
            store,
        )
        return carry

    def line_y(t, carry):
        rows = pl.ds(pl.multiple_of(t * ROWS, ROWS), ROWS)

        def store(at, c, value):
            ty_ref[c, at, rows, :] = value

        march(
            1,
            size_y,
            lambda i: [yl_ref[c, i, rows, :] for c in range(5)],
            lambda i: [q_flat[c, pl.ds(t * (ROWS * size_y) + i, ROWS, stride=size_y), :] for c in range(5)],
            lambda i: [yr_ref[c, i, rows, :] for c in range(5)],
            store,
        )
        return carry

    lax.fori_loop(0, size_y // ROWS, line_x, 0)
    lax.fori_loop(0, size_x // ROWS, line_y, 0)
    step = COURANT / jnp.max(top_ref[...], axis=0, keepdims=True)
    half = size_x // 2

    def last(x, carry):
        for h, part_ref in enumerate((za_ref, zb_ref)):
            for t in range(size_y // ROWS):
                rows = pl.ds(t * ROWS, ROWS)
                for c in range(5):
                    at = h * half + x
                    other = ty_flat[c, pl.ds(t * (ROWS * size_x) + at, ROWS, stride=size_x), :]
                    total = ten_ref[c, at, rows, :] + other + part_ref[c, x, rows, :]
                    ten_ref[c, at, rows, :] = total
                    adv_ref[c, at, rows, :] = q_ref[c, at, rows, :] + step * total
        return carry

    lax.fori_loop(0, half, last, 0)


def prepare(q_ref, xf_ref, xl_ref, yf_ref, yl_ref, top_ref, acc_ref):
    size_x, size_y = q_ref.shape[1], q_ref.shape[2]
    q_flat = q_ref.reshape(5, size_x * size_y, LANES)
    group = pl.program_id(0)

    @pl.when(group == 0)
    def _():
        acc_ref[...] = jnp.zeros_like(acc_ref)

    def speeds(x, top):
        for t in range(size_y // ROWS):
            q = [q_ref[c, x, pl.ds(t * ROWS, ROWS), :] for c in range(5)]
            inv = 1.0 / q[0]
            kinetic = 0.5 * (q[1] * q[1] + q[2] * q[2] + q[3] * q[3]) * inv
            sound_sq = (GAMMA * GAMMA_LESS) * (q[4] - kinetic) * inv
            sound = sound_sq * lax.rsqrt(jnp.maximum(sound_sq, TINY))
            total = (jnp.abs(q[1]) + jnp.abs(q[2]) + jnp.abs(q[3])) * inv + 3.0 * sound
            top = jnp.maximum(top, total)
        return top

    acc_ref[...] = lax.fori_loop(0, size_x, speeds, acc_ref[...])
    for c in range(5):
        for k in range(3):
            xf_ref[c, k] = q_ref[c, k]
            xl_ref[c, k] = q_ref[c, size_x - 3 + k]
            for t in range(size_x // ROWS):
                rows = pl.ds(t * ROWS, ROWS)
                first = t * ROWS * size_y
                yf_ref[c, k, rows, :] = q_flat[c, pl.ds(first + k, ROWS, stride=size_y), :]
                yl_ref[c, k, rows, :] = q_flat[c, pl.ds(first + size_y - 3 + k, ROWS, stride=size_y), :]

    @pl.when(group == pl.num_programs(0) - 1)
    def _():
        top_ref[...] = jnp.full(top_ref.shape, jnp.max(acc_ref[...]), jnp.float32)


def line_scratch(rows):
    return [pltpu.VMEM((count, rows, LANES), jnp.float32) for count in (15, 19, 10, 10)]


def call_prepare(conserved, rows):
    _, size_x, size_y, size_z = conserved.shape

    def spec(first, second):
        return pl.BlockSpec((5, first, second, LANES), lambda g: (0, 0, 0, g))

    layers = jax.ShapeDtypeStruct((5, 3, size_y, size_z), jnp.float32)
    turned = jax.ShapeDtypeStruct((5, 3, size_x, size_z), jnp.float32)
    return pl.pallas_call(
        prepare,
        out_shape=[layers, layers, turned, turned, jax.ShapeDtypeStruct((rows, LANES), jnp.float32)],
        grid=(size_z // LANES,),
        in_specs=[spec(size_x, size_y)],
        out_specs=[spec(3, size_y), spec(3, size_y), spec(3, size_x), spec(3, size_x)]
        + [pl.BlockSpec((rows, LANES), lambda g: (0, 0))],
        scratch_shapes=[pltpu.VMEM((ROWS, LANES), jnp.float32)],
        cost_estimate=pl.CostEstimate(flops=4_000_000, bytes_accessed=2 * conserved.size * 4, transcendentals=0),
        compiler_params=pltpu.CompilerParams(vmem_limit_bytes=12 << 20),
        name="prepare",
    )(conserved)


def call_lanes(flags, conserved, part):
    _, size_x, size_y, size_z = conserved.shape
    chunk = LANES // size_y
    block = (5, chunk, size_y, size_z)
    return pl.pallas_call(
        along_lanes,
        out_shape=jax.ShapeDtypeStruct(block, jnp.float32),
        grid=(1,),
        in_specs=[pl.BlockSpec(memory_space=pltpu.SMEM), pl.BlockSpec(block, lambda _: (0, part, 0, 0))],
        out_specs=pl.BlockSpec(block, lambda _: (0, 0, 0, 0)),
        scratch_shapes=[pltpu.VMEM((10, size_z, LANES), jnp.float32)] + line_scratch(size_z + 8 * ROWS),
        cost_estimate=pl.CostEstimate(flops=60_000_000, bytes_accessed=conserved.size * 4, transcendentals=0),
        compiler_params=pltpu.CompilerParams(vmem_limit_bytes=30 << 20),
        name="along_lanes",
    )(flags, conserved)


def call_others(flags, top, conserved, x_low, x_high, y_low, y_high, parts):
    _, size_x, size_y, size_z = conserved.shape

    def spec(first, second):
        return pl.BlockSpec((5, first, second, LANES), lambda g: (0, 0, 0, g))

    whole = spec(size_x, size_y)
    return pl.pallas_call(
        along_others,
        out_shape=[jax.ShapeDtypeStruct(conserved.shape, jnp.float32)] * 2,
        grid=(size_z // LANES,),
        in_specs=[
            pl.BlockSpec(memory_space=pltpu.SMEM),
            pl.BlockSpec(top.shape, lambda g: (0, 0)),
            whole,
            spec(3, size_y),
            spec(3, size_y),
            spec(3, size_x),
            spec(3, size_x),
            spec(size_x // 2, size_y),
            spec(size_x // 2, size_y),
        ],
        out_specs=[whole, whole],
        scratch_shapes=line_scratch((max(size_x, size_y) + 9) * ROWS)
        + [pltpu.VMEM((5, size_y, size_x, LANES), jnp.float32)],
        cost_estimate=pl.CostEstimate(flops=240_000_000, bytes_accessed=4 * conserved.size * 4, transcendentals=0),
        compiler_params=pltpu.CompilerParams(vmem_limit_bytes=24 << 20),
        name="along_others",
    )(flags, top, conserved, x_low, x_high, y_low, y_high, *parts)


GX = ("ga", "gb")
SPLIT = 4


def neighbours(axis, first, last):
    size = lax.axis_size(axis)
    up = [(i, (i + 1) % size) for i in range(size)]
    down = [(j, i) for i, j in up]
    return lax.ppermute(last, axis, up), lax.ppermute(first, axis, down)


def swap(rows, axes):
    return lax.all_to_all(rows, axes, 0, 0, tiled=True)


def shards(conserved, shock_flags):
    inner, outer = ("gb",), ("ga", "gy")
    count, others = lax.axis_size(inner), lax.axis_size(outer)
    x_first, x_last, y_first, y_last, top = call_prepare(conserved, count)
    x_low, x_high = neighbours(GX, x_first, x_last)
    y_low, y_high = neighbours("gy", y_first, y_last)
    top = swap(top, inner)
    parts = [call_lanes(shock_flags, conserved, 0)]
    top, parts[0] = lax.optimization_barrier((top, parts[0]))
    top = swap(jnp.broadcast_to(jnp.max(top, axis=0, keepdims=True), (others, LANES)), outer)
    parts.append(call_lanes(shock_flags, conserved, 1))
    return call_others(shock_flags, top, conserved, x_low, x_high, y_low, y_high, parts)


def local(conserved, shock_flags, top, x_low, x_high, y_low, y_high):
    x_first, x_last, y_first, y_last, mine = call_prepare(conserved, 16)
    parts = [call_lanes(shock_flags, conserved, h) for h in range(2)]
    return call_others(shock_flags, mine, conserved, x_last, x_first, y_last, y_first, parts)


def solution(mesh):
    devices = mesh.devices
    size_x, size_y = devices.shape
    mesh = jax.sharding.Mesh(devices.reshape(SPLIT, size_x // SPLIT, size_y), (*GX, "gy"))
    spec = P(None, GX, "gy", None)
    return jax.shard_map(
        shards,
        mesh=mesh,
        in_specs=(spec, P(GX, "gy", None)),
        out_specs=(spec, spec),
        check_vma=False,
    )
```

```python
import functools

import jax
import jax.numpy as jnp
from jax import lax
from jax.experimental import pallas as pl
from jax.experimental.pallas import tpu as pltpu
from jax.sharding import PartitionSpec as P

GAMMA = 1.4
GAMMA_LESS = 0.4
COURANT = 0.4
EPSILON = 1e-06
LANES = 128
ROWS = 8
TINY = 1e-37


def cell_values(density, mom, energy, normal):
    inv = 1.0 / density
    inv_half = 0.5 * inv
    half_vel = [m * inv_half for m in mom]
    kinetic = mom[0] * half_vel[0] + mom[1] * half_vel[1] + mom[2] * half_vel[2]
    pressure = GAMMA_LESS * (energy - kinetic)
    total = energy + pressure
    sound_sq = GAMMA * pressure * inv
    sound = sound_sq * lax.rsqrt(jnp.maximum(sound_sq, TINY))
    half_normal = half_vel[normal]
    flux = [0.5 * mom[normal]]
    for other in range(3):
        part = mom[other] * half_normal
        flux.append(part + 0.5 * pressure if other == normal else part)
    flux.append(total * half_normal)
    means = [half_vel[n] for n in pair_order(normal)] + [total * inv_half]
    return flux, means, jnp.abs(half_normal) + 0.5 * sound


def pair_order(normal):
    return [normal] + [other for other in range(3) if other != normal]


def recon_rest(d1, d2, d3, d4):
    t1 = d2 - d1
    t2 = d3 - d2
    t3 = d4 - d3
    d2s = 0.75 * d2
    d3s = 0.75 * d3
    p2 = d2s * d2 + 0.75 * EPSILON
    p3 = d3s * d3 + 0.75 * EPSILON
    r0 = 1.0 / (t1 * (t1 + d2s) + p2)
    r1 = 1.0 / (t2 * (t2 + d2s) + p2)
    r2 = 1.0 / (t3 * (t3 - d3s) + p3)
    z0 = r0 * r0
    z1 = r1 * r1
    z2 = 1.5 * (r2 * r2)
    num = z0 * (t2 - t1) + z2 * (t3 - t2)
    den = z2 + (0.5 * z0 + 3.0 * z1)
    return num * (1.0 / den)


def central_rest(d_flux):
    return [
        (1.0 / 30.0) * ((d_flux[4][c] - d_flux[0][c]) - 7.0 * (d_flux[3][c] - d_flux[1][c]))
        for c in range(5)
    ]


def face_terms(means):
    a, b, e, h = means
    k = 0.5 * (a * a + b * b + e * e)
    s_sq = GAMMA_LESS * (h - k)
    inv_s = lax.rsqrt(s_sq)
    return [a, b, e, h, k, s_sq * inv_s, (0.5 * GAMMA_LESS) * (inv_s * inv_s), 0.5 * inv_s]


def face_order(normal):
    return [0] + [1 + n for n in pair_order(normal)] + [4]


def weno_waves(d_flux, d_state, terms, alpha, normal):
    order = face_order(normal)
    a, b, e, _, k, _, half_g, half_inv = terms

    def project(x):
        x1 = x[1] - a * x[0]
        x2 = x[2] - b * x[0]
        x3 = x[3] - e * x[0]
        y = half_g * (x[4] - a * x1 - b * x2 - e * x3 - k * x[0])
        z = half_inv * x1
        return [y - z, x[0] - (y + y), x2, x3, y + z]

    up = []
    down = []
    for step in range(5):
        scaled = [alpha * d_state[step][c] for c in order]
        flux = [d_flux[step][c] for c in order]
        up.append([f + q for f, q in zip(flux, scaled)] if step < 4 else None)
        down.append([f - q for f, q in zip(flux, scaled)] if step > 0 else None)
    linear = [(up[1][c] - down[3][c]) - (up[2][c] - down[2][c]) for c in range(5)]
    up = [project(x) if x is not None else None for x in up]
    down = [project(x) if x is not None else None for x in down]
    waves = [
        recon_rest(up[0][c], up[1][c], up[2][c], up[3][c])
        - recon_rest(down[4][c], down[3][c], down[2][c], down[1][c])
        for c in range(5)
    ]
    return linear, waves


def weno_rest(linear, waves, terms, normal):
    a, b, e, h, k, s = terms[:6]
    outer = waves[0] + waves[4]
    shared = outer + waves[1]
    swing = s * (waves[4] - waves[0])
    back = [
        shared,
        a * shared + swing,
        b * shared + waves[2],
        e * shared + waves[3],
        h * outer + k * waves[1] + b * waves[2] + e * waves[3] + a * swing,
    ]
    rest = [None] * 5
    for position, component in enumerate(face_order(normal)):
        rest[component] = (1.0 / 6.0) * (linear[position] - back[position])
    return rest


class Line:
    def __init__(self, refs, normal, unit):
        self.v_ref, self.p_ref, self.w_ref, self.f_ref = refs
        self.normal = normal
        self.unit = unit

    def rows(self, i, off=0):
        start = i * ROWS + off * self.unit
        if (off * self.unit) % ROWS == 0 and not isinstance(i, int):
            start = pl.multiple_of(start, ROWS)
        return pl.ds(start, ROWS)

    def cell(self, i, q):
        n = self.normal
        flux, means, wave = cell_values(q[0], q[1:4], q[4], n)
        now = list(q) + flux + means + [wave]
        here, prev = self.rows(i), self.rows(i, -1)
        for v in range(15):
            self.v_ref[v, here, :] = now[v]
        before = [self.v_ref[v, prev, :] for v in range(15)]
        for v in range(10):
            self.p_ref[v, here, :] = now[v] - before[v]
        self.p_ref[10, here, :] = jnp.maximum(now[14], before[14])
        terms = face_terms([now[v] + before[v] for v in range(10, 14)])
        for v in range(8):
            self.p_ref[11 + v, here, :] = terms[v]

    def pair(self, v, j, off=0):
        return self.p_ref[v, self.rows(j, off), :]

    def fluxes(self, j):
        return [[self.pair(5 + c, j, k - 2) for c in range(5)] for k in range(5)]

    def central(self, j, d_flux):
        for c, value in enumerate(central_rest(d_flux)):
            self.f_ref[c, self.rows(j), :] = value

    def waves(self, j, d_flux):
        d_state = [[self.pair(c, j, k - 2) for c in range(5)] for k in range(5)]
        terms = [self.pair(11 + v, j) for v in range(8)]
        alpha = jnp.maximum(jnp.maximum(self.pair(10, j, -2), self.pair(10, j)), self.pair(10, j, 2))
        linear, waves = weno_waves(d_flux, d_state, terms, alpha, self.normal)
        for c in range(5):
            self.w_ref[c, self.rows(j), :] = linear[c]
            self.w_ref[5 + c, self.rows(j), :] = waves[c]

    def face(self, j):
        both = [self.w_ref[c, self.rows(j), :] for c in range(10)]
        terms = [self.pair(11 + v, j) for v in range(6)]
        for c, value in enumerate(weno_rest(both[:5], both[5:], terms, self.normal)):
            self.f_ref[5 + c, self.rows(j), :] = value

    def change(self, j, first):
        here, following = self.rows(j), self.rows(j, 1)
        return [self.f_ref[first + c, here, :] - self.f_ref[first + c, following, :] for c in range(5)]

    def mean_change(self, j, c):
        return self.pair(5 + c, j) + self.pair(5 + c, j, 1)


def along_lanes(first_line, flag_ref, q_ref, out_ref, mark_ref, z_ref, t_ref, v_ref, p_ref, w_ref, f_ref, sems):
    size_x, size_y, width = q_ref.shape[1:]
    q_flat = q_ref.reshape(5, size_x * size_y, width)
    t_flat = t_ref.reshape(width // LANES, 5, LANES, LANES)
    mark_ref[...] = jnp.zeros_like(mark_ref)
    groups = width // LANES
    steps = width // ROWS
    blocks = flag_ref.shape[2]
    per_block = steps // blocks
    assert steps & (steps - 1) == 0 and blocks & (blocks - 1) == 0
    line = Line((v_ref, p_ref, w_ref, f_ref), 2, 1)

    def turn_in(g, carry):
        lanes = pl.ds(pl.multiple_of(g * LANES, LANES), LANES)
        for c in range(5):
            z_ref[c, lanes, :] = q_flat[c, pl.ds(first_line, LANES), lanes].T
        return carry

    def leave(g):
        return pltpu.make_async_copy(t_ref.at[g], out_ref.at[0, g], sems.at[g])

    def turn_out(g):
        lanes = pl.ds(pl.multiple_of(g * LANES, LANES), LANES)
        for c in range(5):
            t_flat[g, c] = z_ref[5 + c, lanes, :].T
        leave(g).start()

    def chunk_of(i):
        return (i + (steps - 2)) & (steps - 1)

    def fetch(i):
        at = chunk_of(i)
        rows = pl.ds(pl.multiple_of(at * ROWS, ROWS), ROWS)
        return [z_ref[c, rows, :] for c in range(5)]


    def flag_of(block):
        return flag_ref[0, 0, (block + blocks) & (blocks - 1)]

    def finish(j, flag):
        j = jnp.maximum(j, 0)
        at = jnp.maximum(j - 2, 0)
        rows = pl.ds(pl.multiple_of(at * ROWS, ROWS), ROWS)
        first = jnp.where(flag > 0, 5, 0)
        for c, value in enumerate(line.change(j, first)):
            z_ref[5 + c, rows, :] = value - line.mean_change(j, c)

    lax.fori_loop(0, groups, turn_in, 0, unroll=True)

    def lead(i, carry):
        line.cell(i, fetch(i))
        return carry

    lax.fori_loop(1, 3 + per_block, lead, 0)

    def body(block, carry):
        start = 2 + block * per_block
        own, one, two = flag_of(block), flag_of(block - 1), flag_of(block - 2)
        steps_here = [start + k for k in range(per_block)]

        def lagging():
            finish(start - per_block - 1, two)
            for i in steps_here[:-1]:
                finish(i - per_block, one)

        @pl.when(own + one + two > 0)
        def _():
            for i in steps_here:
                line.face(i - per_block)
            lagging()
            d_flux = [line.fluxes(i) for i in steps_here]
            for i, d in zip(steps_here, d_flux):
                line.waves(i, d)
            for i, d in zip(steps_here, d_flux):
                line.central(i, d)
            for i in steps_here:
                line.cell(i + per_block + 1, fetch(i + per_block + 1))

        @pl.when(own + one + two <= 0)
        def _():
            lagging()
            for i in steps_here:
                line.central(i, line.fluxes(i))
            for i in steps_here:
                line.cell(i + per_block + 1, fetch(i + per_block + 1))

        return carry

    per_group = blocks // groups

    def lane_group(g, carry):
        lax.fori_loop(g * per_group, (g + 1) * per_group, body, 0)

        @pl.when(g > 0)
        def _():
            turn_out(g - 1)

        return carry

    lax.fori_loop(0, groups, lane_group, 0)
    for k in range(per_block):
        line.face(steps + 2 - per_block + k)
    for c in range(10):
        f_ref[c, pl.ds(ROWS * (steps + 2), ROWS), :] = f_ref[c, pl.ds(2 * ROWS, ROWS), :]
    for i in range(steps + 1 - per_block, steps + 2):
        finish(i, flag_of((i - 2) // per_block))
    turn_out(groups - 1)
    for g in range(groups):
        leave(g).wait()


def along_others(
    flag_ref, top_ref, q_ref, xl_ref, xr_ref, yl_ref, yr_ref, za_ref, zb_ref, adv_ref, ten_ref, v_ref, p_ref, w_ref, f_ref, ty_ref
):
    group = pl.program_id(0)
    size_x, size_y = q_ref.shape[1], q_ref.shape[2]
    q_flat = q_ref.reshape(5, size_x * size_y, LANES)
    ty_flat = ty_ref.reshape(5, size_y * size_x, LANES)
    per_group = flag_ref.shape[2] // pl.num_programs(0)
    edge = LANES // per_group
    lane_block = lax.broadcasted_iota(jnp.int32, (ROWS, LANES), 1) // edge
    marks = jnp.zeros((ROWS, LANES), jnp.int32)
    some = jnp.int32(0)
    for b in range(per_group):
        flag = flag_ref[0, 0, group * per_group + b]
        marks = jnp.where(lane_block == b, flag, marks)
        some = jnp.maximum(some, flag)
    shock = marks > 0

    def march(normal, count, left, middle, right, store):
        line = Line((v_ref, p_ref, w_ref, f_ref), normal, ROWS)

        def from_left(i, carry):
            line.cell(1 + i, left(i))
            return carry

        def from_middle(i, carry):
            line.cell(4 + i, middle(i))
            return carry

        lax.fori_loop(0, 3, from_left, 0, unroll=True)
        lax.fori_loop(0, 4, from_middle, 0, unroll=True)

        def ahead(j):
            inner = j - 1 < count
            near = middle(jnp.minimum(j - 1, count - 1))
            far = right(jnp.clip(j - 1 - count, 0, 2))
            line.cell(j + 3, [jnp.where(inner, n, f) for n, f in zip(near, far)])

        def finish(j, sharp):
            at = jnp.maximum(j - 4, 0)
            change = line.change(j, 0)
            if sharp:
                change = [jnp.where(shock, w, c) for w, c in zip(line.change(j, 5), change)]
            for c in range(5):
                store(at, c, change[c] - line.mean_change(j, c))

        @pl.when(some > 0)
        def _():
            def waves(steps):
                d_flux = [line.fluxes(j) for j in steps]
                for j, d in zip(steps, d_flux):
                    line.waves(j, d)
                for j, d in zip(steps, d_flux):
                    line.central(j, d)

            def two(n, carry):
                j = 4 + 2 * n
                for k in (2, 1):
                    line.face(j - k)
                for k in (3, 2):
                    finish(j - k, True)
                waves([j, j + 1])
                for k in (1, 2):
                    ahead(j + k)
                return carry

            pairs = (count + 1) // 2
            lax.fori_loop(0, pairs, two, 0)
            left_over = list(range(4 + 2 * pairs, 5 + count))
            waves(left_over)
            for j in [2 + 2 * pairs, 3 + 2 * pairs] + left_over:
                line.face(j)
            for j in range(1 + 2 * pairs, 4 + count):
                finish(j, True)

        @pl.when(some <= 0)
        def _():
            def body(j, carry):
                ahead(j)
                line.central(j, line.fluxes(j))
                finish(j - 1, False)
                return carry

            lax.fori_loop(4, 5 + count, body, 0)

    def line_x(t, carry):
        rows = pl.ds(pl.multiple_of(t * ROWS, ROWS), ROWS)

        def store(at, c, value):
            ten_ref[c, at, rows, :] = value

        march(
            0,
            size_x,
            lambda i: [xl_ref[c, i, rows, :] for c in range(5)],
            lambda i: [q_ref[c, i, rows, :] for c in range(5)],
            lambda i: [xr_ref[c, i, rows, :] for c in range(5)],
            store,
        )
        return carry

    def line_y(t, carry):
        rows = pl.ds(pl.multiple_of(t * ROWS, ROWS), ROWS)

        def store(at, c, value):
            ty_ref[c, at, rows, :] = value

        march(
            1,
            size_y,
            lambda i: [yl_ref[c, i, rows, :] for c in range(5)],
            lambda i: [q_flat[c, pl.ds(t * (ROWS * size_y) + i, ROWS, stride=size_y), :] for c in range(5)],
            lambda i: [yr_ref[c, i, rows, :] for c in range(5)],
            store,
        )
        return carry

    lax.fori_loop(0, size_y // ROWS, line_x, 0)
    lax.fori_loop(0, size_x // ROWS, line_y, 0)
    step = COURANT / jnp.max(top_ref[...], axis=0, keepdims=True)
    half = size_x // 2

    def last(x, carry):
        for h, part_ref in enumerate((za_ref, zb_ref)):
            for t in range(size_y // ROWS):
                rows = pl.ds(t * ROWS, ROWS)
                for c in range(5):
                    at = h * half + x
                    other = ty_flat[c, pl.ds(t * (ROWS * size_x) + at, ROWS, stride=size_x), :]
                    total = ten_ref[c, at, rows, :] + other + part_ref[c, x, rows, :]
                    ten_ref[c, at, rows, :] = total
                    adv_ref[c, at, rows, :] = q_ref[c, at, rows, :] + step * total
        return carry

    lax.fori_loop(0, half, last, 0)


def prepare(q_ref, xf_ref, xl_ref, yf_ref, yl_ref, top_ref):
    size_x, size_y, width = q_ref.shape[1:]

    def speeds(x, top):
        for t in range(size_y // ROWS):
            for g in range(width // LANES):
                q = [q_ref[c, x, pl.ds(t * ROWS, ROWS), pl.ds(g * LANES, LANES)] for c in range(5)]
                inv = 1.0 / q[0]
                kinetic = 0.5 * (q[1] * q[1] + q[2] * q[2] + q[3] * q[3]) * inv
                sound_sq = (GAMMA * GAMMA_LESS) * (q[4] - kinetic) * inv
                sound = sound_sq * lax.rsqrt(jnp.maximum(sound_sq, TINY))
                total = (jnp.abs(q[1]) + jnp.abs(q[2]) + jnp.abs(q[3])) * inv + 3.0 * sound
                top = jnp.maximum(top, total)
        for c in range(5):
            for k in range(3):
                yf_ref[c, k, pl.ds(x, 1), :] = q_ref[c, x, pl.ds(k, 1), :]
                yl_ref[c, k, pl.ds(x, 1), :] = q_ref[c, x, pl.ds(size_y - 3 + k, 1), :]
        return top

    top = lax.fori_loop(0, size_x, speeds, jnp.zeros((ROWS, LANES), jnp.float32))
    top_ref[...] = jnp.full(top_ref.shape, jnp.max(top), jnp.float32)
    for c in range(5):
        for k in range(3):
            xf_ref[c, k] = q_ref[c, k]
            xl_ref[c, k] = q_ref[c, size_x - 3 + k]


def line_scratch(rows):
    return [pltpu.VMEM((count, rows, LANES), jnp.float32) for count in (15, 19, 10, 10)]


WHOLE = pl.BlockSpec(memory_space=pltpu.VMEM)
SPARE = 28


def call_prepare(conserved, rows):
    _, size_x, size_y, size_z = conserved.shape
    layers = jax.ShapeDtypeStruct((5, 3, size_y, size_z), jnp.float32)
    turned = jax.ShapeDtypeStruct((5, 3, size_x, size_z), jnp.float32)
    return pl.pallas_call(
        prepare,
        out_shape=[layers, layers, turned, turned, jax.ShapeDtypeStruct((rows, LANES), jnp.float32)],
        in_specs=[WHOLE],
        out_specs=[WHOLE] * 5,
        cost_estimate=pl.CostEstimate(flops=4_000_000, bytes_accessed=2 * conserved.size * 4, transcendentals=0),
        compiler_params=pltpu.CompilerParams(vmem_limit_bytes=12 << 20),
        name="prepare",
    )(conserved)


def call_lanes(flags, conserved, part):
    _, size_x, size_y, size_z = conserved.shape
    block = (size_z // LANES, 5, LANES // size_y, size_y, LANES)
    return pl.pallas_call(
        functools.partial(along_lanes, part * LANES),
        out_shape=[jax.ShapeDtypeStruct((SPARE, *block), jnp.float32), jax.ShapeDtypeStruct((ROWS, LANES), jnp.float32)],
        in_specs=[pl.BlockSpec(memory_space=pltpu.SMEM), WHOLE],
        out_specs=[pl.BlockSpec(memory_space=pl.ANY), WHOLE],
        scratch_shapes=[pltpu.VMEM((10, size_z, LANES), jnp.float32), pltpu.VMEM(block, jnp.float32)]
        + line_scratch(size_z + 8 * ROWS)
        + [pltpu.SemaphoreType.DMA((size_z // LANES,))],
        cost_estimate=pl.CostEstimate(flops=60_000_000, bytes_accessed=conserved.size * 4, transcendentals=0),
        compiler_params=pltpu.CompilerParams(vmem_limit_bytes=30 << 20),
        name="along_lanes",
    )(flags, conserved)


def call_others(flags, top, conserved, x_low, x_high, y_low, y_high, parts):
    _, size_x, size_y, size_z = conserved.shape

    def spec(first, second):
        return pl.BlockSpec((5, first, second, LANES), lambda g: (0, 0, 0, g))

    whole = spec(size_x, size_y)
    part = pl.BlockSpec((pl.Squeezed(), pl.Squeezed(), 5, size_x // 2, size_y, LANES), lambda g: (0, g, 0, 0, 0, 0))
    return pl.pallas_call(
        along_others,
        out_shape=[jax.ShapeDtypeStruct(conserved.shape, jnp.float32)] * 2,
        grid=(size_z // LANES,),
        in_specs=[
            pl.BlockSpec(memory_space=pltpu.SMEM),
            pl.BlockSpec(top.shape, lambda g: (0, 0)),
            whole,
            spec(3, size_y),
            spec(3, size_y),
            spec(3, size_x),
            spec(3, size_x),
            part,
            part,
        ],
        out_specs=[whole, whole],
        scratch_shapes=line_scratch((max(size_x, size_y) + 9) * ROWS)
        + [pltpu.VMEM((5, size_y, size_x, LANES), jnp.float32)],
        cost_estimate=pl.CostEstimate(flops=240_000_000, bytes_accessed=4 * conserved.size * 4, transcendentals=0),
        compiler_params=pltpu.CompilerParams(vmem_limit_bytes=24 << 20),
        name="along_others",
    )(flags, top, conserved, x_low, x_high, y_low, y_high, *parts)


GX = ("ga", "gb")
SPLIT = 4


def neighbours(axis, first, last):
    size = lax.axis_size(axis)
    up = [(i, (i + 1) % size) for i in range(size)]
    down = [(j, i) for i, j in up]
    return lax.ppermute(last, axis, up), lax.ppermute(first, axis, down)


def swap(rows, axes):
    return lax.all_to_all(rows, axes, 0, 0, tiled=True)


def shards(conserved, shock_flags):
    inner, outer = ("gb",), ("ga", "gy")
    count, others = lax.axis_size(inner), lax.axis_size(outer)
    x_first, x_last, y_first, y_last, top = call_prepare(conserved, count)
    x_low, x_high = neighbours(GX, x_first, x_last)
    y_low, y_high = neighbours("gy", y_first, y_last)
    top = swap(top, inner)
    first, mark = call_lanes(shock_flags, conserved, 0)
    top = jnp.maximum(jnp.max(top, axis=0, keepdims=True), mark[:1])
    top = swap(jnp.broadcast_to(top, (others, LANES)), outer)
    second, _ = call_lanes(shock_flags, conserved, 1)
    return call_others(shock_flags, top, conserved, x_low, x_high, y_low, y_high, (first, second))


def local(conserved, shock_flags, top, x_low, x_high, y_low, y_high):
    x_first, x_last, y_first, y_last, mine = call_prepare(conserved, 16)
    parts = [call_lanes(shock_flags, conserved, h)[0] for h in range(2)]
    return call_others(shock_flags, mine, conserved, x_last, x_first, y_last, y_first, parts)


def solution(mesh):
    devices = mesh.devices
    size_x, size_y = devices.shape
    mesh = jax.sharding.Mesh(devices.reshape(SPLIT, size_x // SPLIT, size_y), (*GX, "gy"))
    spec = P(None, GX, "gy", None)
    return jax.shard_map(
        shards,
        mesh=mesh,
        in_specs=(spec, P(GX, "gy", None)),
        out_specs=(spec, spec),
        check_vma=False,
    )
```

```python
import functools

import jax
import jax.numpy as jnp
from jax import lax
from jax.experimental import pallas as pl
from jax.experimental.pallas import tpu as pltpu
from jax.sharding import PartitionSpec as P

GAMMA = 1.4
GAMMA_LESS = 0.4
COURANT = 0.4
EPSILON = 1e-06
LANES = 128
ROWS = 8
TINY = 1e-37


def cell_values(density, mom, energy, normal):
    inv = 1.0 / density
    inv_half = 0.5 * inv
    half_vel = [m * inv_half for m in mom]
    kinetic = mom[0] * half_vel[0] + mom[1] * half_vel[1] + mom[2] * half_vel[2]
    pressure = GAMMA_LESS * (energy - kinetic)
    total = energy + pressure
    sound_sq = GAMMA * pressure * inv
    sound = sound_sq * lax.rsqrt(jnp.maximum(sound_sq, TINY))
    half_normal = half_vel[normal]
    flux = [0.5 * mom[normal]]
    for other in range(3):
        part = mom[other] * half_normal
        flux.append(part + 0.5 * pressure if other == normal else part)
    flux.append(total * half_normal)
    means = [half_vel[n] for n in pair_order(normal)] + [total * inv_half]
    return flux, means, jnp.abs(half_normal) + 0.5 * sound


def pair_order(normal):
    return [normal] + [other for other in range(3) if other != normal]


def recon_rest(d1, d2, d3, d4):
    t1 = d2 - d1
    t2 = d3 - d2
    t3 = d4 - d3
    d2s = 0.75 * d2
    d3s = 0.75 * d3
    p2 = d2s * d2 + 0.75 * EPSILON
    p3 = d3s * d3 + 0.75 * EPSILON
    r0 = 1.0 / (t1 * (t1 + d2s) + p2)
    r1 = 1.0 / (t2 * (t2 + d2s) + p2)
    r2 = 1.0 / (t3 * (t3 - d3s) + p3)
    z0 = r0 * r0
    z1 = r1 * r1
    z2 = 1.5 * (r2 * r2)
    num = z0 * (t2 - t1) + z2 * (t3 - t2)
    den = z2 + (0.5 * z0 + 3.0 * z1)
    return num * (1.0 / den)


def central_rest(d_flux):
    return [
        (1.0 / 30.0) * ((d_flux[4][c] - d_flux[0][c]) - 7.0 * (d_flux[3][c] - d_flux[1][c]))
        for c in range(5)
    ]


def face_terms(means):
    a, b, e, h = means
    k = 0.5 * (a * a + b * b + e * e)
    s_sq = GAMMA_LESS * (h - k)
    inv_s = lax.rsqrt(s_sq)
    return [a, b, e, h, k, s_sq * inv_s, (0.5 * GAMMA_LESS) * (inv_s * inv_s), 0.5 * inv_s]


def face_order(normal):
    return [0] + [1 + n for n in pair_order(normal)] + [4]


def weno_waves(d_flux, d_state, terms, alpha, normal):
    order = face_order(normal)
    a, b, e, _, k, _, half_g, half_inv = terms

    def project(x):
        x1 = x[1] - a * x[0]
        x2 = x[2] - b * x[0]
        x3 = x[3] - e * x[0]
        y = half_g * (x[4] - a * x1 - b * x2 - e * x3 - k * x[0])
        z = half_inv * x1
        return [y - z, x[0] - (y + y), x2, x3, y + z]

    up = []
    down = []
    for step in range(5):
        scaled = [alpha * d_state[step][c] for c in order]
        flux = [d_flux[step][c] for c in order]
        up.append([f + q for f, q in zip(flux, scaled)] if step < 4 else None)
        down.append([f - q for f, q in zip(flux, scaled)] if step > 0 else None)
    linear = [(up[1][c] - down[3][c]) - (up[2][c] - down[2][c]) for c in range(5)]
    up = [project(x) if x is not None else None for x in up]
    down = [project(x) if x is not None else None for x in down]
    waves = [
        recon_rest(up[0][c], up[1][c], up[2][c], up[3][c])
        - recon_rest(down[4][c], down[3][c], down[2][c], down[1][c])
        for c in range(5)
    ]
    return linear, waves


def weno_rest(linear, waves, terms, normal):
    a, b, e, h, k, s = terms[:6]
    outer = waves[0] + waves[4]
    shared = outer + waves[1]
    swing = s * (waves[4] - waves[0])
    back = [
        shared,
        a * shared + swing,
        b * shared + waves[2],
        e * shared + waves[3],
        h * outer + k * waves[1] + b * waves[2] + e * waves[3] + a * swing,
    ]
    rest = [None] * 5
    for position, component in enumerate(face_order(normal)):
        rest[component] = (1.0 / 6.0) * (linear[position] - back[position])
    return rest


class Line:
    def __init__(self, refs, normal, unit):
        self.v_ref, self.p_ref, self.w_ref, self.f_ref = refs
        self.normal = normal
        self.unit = unit

    def rows(self, i, off=0):
        start = i * ROWS + off * self.unit
        if (off * self.unit) % ROWS == 0 and not isinstance(i, int):
            start = pl.multiple_of(start, ROWS)
        return pl.ds(start, ROWS)

    def cell(self, i, q):
        n = self.normal
        flux, means, wave = cell_values(q[0], q[1:4], q[4], n)
        now = list(q) + flux + means + [wave]
        here, prev = self.rows(i), self.rows(i, -1)
        for v in range(15):
            self.v_ref[v, here, :] = now[v]
        before = [self.v_ref[v, prev, :] for v in range(15)]
        for v in range(10):
            self.p_ref[v, here, :] = now[v] - before[v]
        self.p_ref[10, here, :] = jnp.maximum(now[14], before[14])
        terms = face_terms([now[v] + before[v] for v in range(10, 14)])
        for v in range(8):
            self.p_ref[11 + v, here, :] = terms[v]

    def pair(self, v, j, off=0):
        return self.p_ref[v, self.rows(j, off), :]

    def fluxes(self, j):
        return [[self.pair(5 + c, j, k - 2) for c in range(5)] for k in range(5)]

    def central(self, j, d_flux):
        for c, value in enumerate(central_rest(d_flux)):
            self.f_ref[c, self.rows(j), :] = value

    def waves(self, j, d_flux):
        d_state = [[self.pair(c, j, k - 2) for c in range(5)] for k in range(5)]
        terms = [self.pair(11 + v, j) for v in range(8)]
        alpha = jnp.maximum(jnp.maximum(self.pair(10, j, -2), self.pair(10, j)), self.pair(10, j, 2))
        linear, waves = weno_waves(d_flux, d_state, terms, alpha, self.normal)
        for c in range(5):
            self.w_ref[c, self.rows(j), :] = linear[c]
            self.w_ref[5 + c, self.rows(j), :] = waves[c]

    def face(self, j):
        both = [self.w_ref[c, self.rows(j), :] for c in range(10)]
        terms = [self.pair(11 + v, j) for v in range(6)]
        for c, value in enumerate(weno_rest(both[:5], both[5:], terms, self.normal)):
            self.f_ref[5 + c, self.rows(j), :] = value

    def change(self, j, first):
        here, following = self.rows(j), self.rows(j, 1)
        return [self.f_ref[first + c, here, :] - self.f_ref[first + c, following, :] for c in range(5)]

    def mean_change(self, j, c):
        return self.pair(5 + c, j) + self.pair(5 + c, j, 1)


def along_lanes(flag_ref, q_ref, out_ref, z_ref, t_ref, v_ref, p_ref, w_ref, f_ref, sems):
    size_x, size_y, width = q_ref.shape[1:]
    q_flat = q_ref.reshape(5, size_x * size_y, width)
    parts = size_x * size_y // LANES
    t_flat = t_ref.reshape(parts * (width // LANES), 5, LANES, LANES)
    groups = width // LANES
    steps = width // ROWS
    blocks = flag_ref.shape[2]
    per_block = steps // blocks
    assert steps & (steps - 1) == 0 and blocks & (blocks - 1) == 0
    line = Line((v_ref, p_ref, w_ref, f_ref), 2, 1)

    def turn_in(part, g):
        lines = pl.ds(pl.multiple_of(part * LANES, LANES), LANES)
        lanes = pl.ds(pl.multiple_of(g * LANES, LANES), LANES)
        for c in range(5):
            z_ref[c, lanes, :] = q_flat[c, lines, lanes].T

    def leave(slot):
        return pltpu.make_async_copy(t_ref.at[slot], out_ref.at[0, slot], sems.at[slot])

    def turn_out(part, g):
        lanes = pl.ds(pl.multiple_of(g * LANES, LANES), LANES)
        slot = part * groups + g
        for c in range(5):
            t_flat[slot, c] = z_ref[5 + c, lanes, :].T
        leave(slot).start()

    def chunk_of(i):
        return (i + (steps - 2)) & (steps - 1)

    def fetch(i):
        at = chunk_of(i)
        rows = pl.ds(pl.multiple_of(at * ROWS, ROWS), ROWS)
        return [z_ref[c, rows, :] for c in range(5)]


    def flag_of(block):
        return flag_ref[0, 0, (block + blocks) & (blocks - 1)]

    def finish(j, flag):
        j = jnp.maximum(j, 0)
        at = jnp.maximum(j - 2, 0)
        rows = pl.ds(pl.multiple_of(at * ROWS, ROWS), ROWS)
        first = jnp.where(flag > 0, 5, 0)
        for c, value in enumerate(line.change(j, first)):
            z_ref[5 + c, rows, :] = value - line.mean_change(j, c)

    def lead(i, carry):
        line.cell(i, fetch(i))
        return carry

    def body(block, carry):
        start = 2 + block * per_block
        own, one, two = flag_of(block), flag_of(block - 1), flag_of(block - 2)
        steps_here = [start + k for k in range(per_block)]

        def lagging():
            finish(start - per_block - 1, two)
            for i in steps_here[:-1]:
                finish(i - per_block, one)

        @pl.when(own + one + two > 0)
        def _():
            for i in steps_here:
                line.face(i - per_block)
            lagging()
            d_flux = [line.fluxes(i) for i in steps_here]
            for i, d in zip(steps_here, d_flux):
                line.waves(i, d)
            for i, d in zip(steps_here, d_flux):
                line.central(i, d)
            for i in steps_here:
                line.cell(i + per_block + 1, fetch(i + per_block + 1))

        @pl.when(own + one + two <= 0)
        def _():
            lagging()
            for i in steps_here:
                line.central(i, line.fluxes(i))
            for i in steps_here:
                line.cell(i + per_block + 1, fetch(i + per_block + 1))

        return carry

    per_group = blocks // groups

    def one_part(part, carry):
        for g in range(groups):
            turn_in(part, g)
        lax.fori_loop(1, 3 + per_block, lead, 0)

        def lane_group(g, carry):
            lax.fori_loop(g * per_group, (g + 1) * per_group, body, 0)

            @pl.when(g > 0)
            def _():
                turn_out(part, g - 1)

            return carry

        lax.fori_loop(0, groups, lane_group, 0)
        for k in range(per_block):
            line.face(steps + 2 - per_block + k)
        for c in range(10):
            f_ref[c, pl.ds(ROWS * (steps + 2), ROWS), :] = f_ref[c, pl.ds(2 * ROWS, ROWS), :]
        for i in range(steps + 1 - per_block, steps + 2):
            finish(i, flag_of((i - 2) // per_block))
        turn_out(part, groups - 1)
        return carry

    lax.fori_loop(0, parts, one_part, 0)
    for slot in range(parts * groups):
        leave(slot).wait()


def along_others(
    flag_ref, top_ref, q_ref, xl_ref, xr_ref, yl_ref, yr_ref, za_ref, zb_ref, adv_ref, ten_ref, v_ref, p_ref, w_ref, f_ref, ty_ref
):
    group = pl.program_id(0)
    size_x, size_y = q_ref.shape[1], q_ref.shape[2]
    q_flat = q_ref.reshape(5, size_x * size_y, LANES)
    ty_flat = ty_ref.reshape(5, size_y * size_x, LANES)
    per_group = flag_ref.shape[2] // pl.num_programs(0)
    edge = LANES // per_group
    lane_block = lax.broadcasted_iota(jnp.int32, (ROWS, LANES), 1) // edge
    marks = jnp.zeros((ROWS, LANES), jnp.int32)
    some = jnp.int32(0)
    for b in range(per_group):
        flag = flag_ref[0, 0, group * per_group + b]
        marks = jnp.where(lane_block == b, flag, marks)
        some = jnp.maximum(some, flag)
    shock = marks > 0

    def march(normal, count, left, middle, right, store):
        line = Line((v_ref, p_ref, w_ref, f_ref), normal, ROWS)

        def from_left(i, carry):
            line.cell(1 + i, left(i))
            return carry

        def from_middle(i, carry):
            line.cell(4 + i, middle(i))
            return carry

        lax.fori_loop(0, 3, from_left, 0, unroll=True)
        lax.fori_loop(0, 4, from_middle, 0, unroll=True)

        def ahead(j):
            inner = j - 1 < count
            near = middle(jnp.minimum(j - 1, count - 1))
            far = right(jnp.clip(j - 1 - count, 0, 2))
            line.cell(j + 3, [jnp.where(inner, n, f) for n, f in zip(near, far)])

        def finish(j, sharp):
            at = jnp.maximum(j - 4, 0)
            change = line.change(j, 0)
            if sharp:
                change = [jnp.where(shock, w, c) for w, c in zip(line.change(j, 5), change)]
            for c in range(5):
                store(at, c, change[c] - line.mean_change(j, c))

        @pl.when(some > 0)
        def _():
            def waves(steps):
                d_flux = [line.fluxes(j) for j in steps]
                for j, d in zip(steps, d_flux):
                    line.waves(j, d)
                for j, d in zip(steps, d_flux):
                    line.central(j, d)

            def two(n, carry):
                j = 4 + 2 * n
                for k in (2, 1):
                    line.face(j - k)
                for k in (3, 2):
                    finish(j - k, True)
                waves([j, j + 1])
                for k in (1, 2):
                    ahead(j + k)
                return carry

            pairs = (count + 1) // 2
            lax.fori_loop(0, pairs, two, 0)
            left_over = list(range(4 + 2 * pairs, 5 + count))
            waves(left_over)
            for j in [2 + 2 * pairs, 3 + 2 * pairs] + left_over:
                line.face(j)
            for j in range(1 + 2 * pairs, 4 + count):
                finish(j, True)

        @pl.when(some <= 0)
        def _():
            def body(j, carry):
                ahead(j)
                line.central(j, line.fluxes(j))
                finish(j - 1, False)
                return carry

            lax.fori_loop(4, 5 + count, body, 0)

    def line_x(t, carry):
        rows = pl.ds(pl.multiple_of(t * ROWS, ROWS), ROWS)

        def store(at, c, value):
            ten_ref[c, at, rows, :] = value

        march(
            0,
            size_x,
            lambda i: [xl_ref[c, i, rows, :] for c in range(5)],
            lambda i: [q_ref[c, i, rows, :] for c in range(5)],
            lambda i: [xr_ref[c, i, rows, :] for c in range(5)],
            store,
        )
        return carry

    def line_y(t, carry):
        rows = pl.ds(pl.multiple_of(t * ROWS, ROWS), ROWS)

        def store(at, c, value):
            ty_ref[c, at, rows, :] = value

        march(
            1,
            size_y,
            lambda i: [yl_ref[c, i, rows, :] for c in range(5)],
            lambda i: [q_flat[c, pl.ds(t * (ROWS * size_y) + i, ROWS, stride=size_y), :] for c in range(5)],
            lambda i: [yr_ref[c, i, rows, :] for c in range(5)],
            store,
        )
        return carry

    lax.fori_loop(0, size_y // ROWS, line_x, 0)
    lax.fori_loop(0, size_x // ROWS, line_y, 0)
    step = COURANT / jnp.max(top_ref[...], axis=0, keepdims=True)
    half = size_x // 2

    def last(x, carry):
        for h, part_ref in enumerate((za_ref, zb_ref)):
            for t in range(size_y // ROWS):
                rows = pl.ds(t * ROWS, ROWS)
                for c in range(5):
                    at = h * half + x
                    other = ty_flat[c, pl.ds(t * (ROWS * size_x) + at, ROWS, stride=size_x), :]
                    total = ten_ref[c, at, rows, :] + other + part_ref[c, x, rows, :]
                    ten_ref[c, at, rows, :] = total
                    adv_ref[c, at, rows, :] = q_ref[c, at, rows, :] + step * total
        return carry

    lax.fori_loop(0, half, last, 0)


def prepare(q_ref, xf_ref, xl_ref, yf_ref, yl_ref, top_ref):
    size_x, size_y, width = q_ref.shape[1:]

    def speeds(x, top):
        for t in range(size_y // ROWS):
            for g in range(width // LANES):
                q = [q_ref[c, x, pl.ds(t * ROWS, ROWS), pl.ds(g * LANES, LANES)] for c in range(5)]
                inv = 1.0 / q[0]
                kinetic = 0.5 * (q[1] * q[1] + q[2] * q[2] + q[3] * q[3]) * inv
                sound_sq = (GAMMA * GAMMA_LESS) * (q[4] - kinetic) * inv
                sound = sound_sq * lax.rsqrt(jnp.maximum(sound_sq, TINY))
                total = (jnp.abs(q[1]) + jnp.abs(q[2]) + jnp.abs(q[3])) * inv + 3.0 * sound
                top = jnp.maximum(top, total)
        for c in range(5):
            for k in range(3):
                yf_ref[c, k, pl.ds(x, 1), :] = q_ref[c, x, pl.ds(k, 1), :]
                yl_ref[c, k, pl.ds(x, 1), :] = q_ref[c, x, pl.ds(size_y - 3 + k, 1), :]
        return top

    top = lax.fori_loop(0, size_x, speeds, jnp.zeros((ROWS, LANES), jnp.float32))
    top_ref[...] = jnp.full(top_ref.shape, jnp.max(top), jnp.float32)
    for c in range(5):
        for k in range(3):
            xf_ref[c, k] = q_ref[c, k]
            xl_ref[c, k] = q_ref[c, size_x - 3 + k]


def line_scratch(rows):
    return [pltpu.VMEM((count, rows, LANES), jnp.float32) for count in (15, 19, 10, 10)]


WHOLE = pl.BlockSpec(memory_space=pltpu.VMEM)
SPARE = 14


def call_prepare(conserved, rows):
    _, size_x, size_y, size_z = conserved.shape
    layers = jax.ShapeDtypeStruct((5, 3, size_y, size_z), jnp.float32)
    turned = jax.ShapeDtypeStruct((5, 3, size_x, size_z), jnp.float32)
    return pl.pallas_call(
        prepare,
        out_shape=[layers, layers, turned, turned, jax.ShapeDtypeStruct((rows, LANES), jnp.float32)],
        in_specs=[WHOLE],
        out_specs=[WHOLE] * 5,
        cost_estimate=pl.CostEstimate(flops=4_000_000, bytes_accessed=2 * conserved.size * 4, transcendentals=0),
        compiler_params=pltpu.CompilerParams(vmem_limit_bytes=12 << 20),
        name="prepare",
    )(conserved)


def call_lanes(flags, conserved):
    _, size_x, size_y, size_z = conserved.shape
    parts = size_x * size_y // LANES
    block = (parts * (size_z // LANES), 5, LANES // size_y, size_y, LANES)
    return pl.pallas_call(
        along_lanes,
        out_shape=jax.ShapeDtypeStruct((SPARE, *block), jnp.float32),
        in_specs=[pl.BlockSpec(memory_space=pltpu.SMEM), WHOLE],
        out_specs=pl.BlockSpec(memory_space=pl.ANY),
        scratch_shapes=[pltpu.VMEM((10, size_z, LANES), jnp.float32), pltpu.VMEM(block, jnp.float32)]
        + line_scratch(size_z + 8 * ROWS)
        + [pltpu.SemaphoreType.DMA((block[0],))],
        cost_estimate=pl.CostEstimate(flops=120_000_000, bytes_accessed=2 * conserved.size * 4, transcendentals=0),
        compiler_params=pltpu.CompilerParams(vmem_limit_bytes=30 << 20),
        name="along_lanes",
    )(flags, conserved)


def call_others(flags, top, conserved, x_low, x_high, y_low, y_high, part):
    _, size_x, size_y, size_z = conserved.shape

    def spec(first, second):
        return pl.BlockSpec((5, first, second, LANES), lambda g: (0, 0, 0, g))

    whole = spec(size_x, size_y)
    groups = size_z // LANES

    def half(h):
        block = (pl.Squeezed(), pl.Squeezed(), 5, size_x // 2, size_y, LANES)
        return pl.BlockSpec(block, lambda g: (0, h * groups + g, 0, 0, 0, 0))

    return pl.pallas_call(
        along_others,
        out_shape=[jax.ShapeDtypeStruct(conserved.shape, jnp.float32)] * 2,
        grid=(size_z // LANES,),
        in_specs=[
            pl.BlockSpec(memory_space=pltpu.SMEM),
            pl.BlockSpec(top.shape, lambda g: (0, 0)),
            whole,
            spec(3, size_y),
            spec(3, size_y),
            spec(3, size_x),
            spec(3, size_x),
            half(0),
            half(1),
        ],
        out_specs=[whole, whole],
        scratch_shapes=line_scratch((max(size_x, size_y) + 9) * ROWS)
        + [pltpu.VMEM((5, size_y, size_x, LANES), jnp.float32)],
        cost_estimate=pl.CostEstimate(flops=240_000_000, bytes_accessed=4 * conserved.size * 4, transcendentals=0),
        compiler_params=pltpu.CompilerParams(vmem_limit_bytes=24 << 20),
        name="along_others",
    )(flags, top, conserved, x_low, x_high, y_low, y_high, part, part)


def neighbours(axis, first, last):
    size = lax.axis_size(axis)
    up = [(i, (i + 1) % size) for i in range(size)]
    down = [(j, i) for i, j in up]
    return lax.ppermute(last, axis, up), lax.ppermute(first, axis, down)


def shards(conserved, shock_flags):
    everyone = ("gx", "gy")
    x_first, x_last, y_first, y_last, top = call_prepare(conserved, lax.axis_size(everyone))
    x_low, x_high = neighbours("gx", x_first, x_last)
    y_low, y_high = neighbours("gy", y_first, y_last)
    top = lax.all_to_all(top, everyone, 0, 0, tiled=True)
    part = call_lanes(shock_flags, conserved)
    return call_others(shock_flags, top, conserved, x_low, x_high, y_low, y_high, part)


def local(conserved, shock_flags, top, x_low, x_high, y_low, y_high):
    x_first, x_last, y_first, y_last, mine = call_prepare(conserved, 256)
    part = call_lanes(shock_flags, conserved)
    return call_others(shock_flags, mine, conserved, x_last, x_first, y_last, y_first, part)


def solution(mesh):
    spec = P(None, "gx", "gy", None)
    return jax.shard_map(
        shards,
        mesh=mesh,
        in_specs=(spec, P("gx", "gy", None)),
        out_specs=(spec, spec),
        check_vma=False,
    )
```

```python
import functools

import jax
import jax.numpy as jnp
from jax import lax
from jax.experimental import pallas as pl
from jax.experimental.pallas import tpu as pltpu
from jax.sharding import PartitionSpec as P

GAMMA = 1.4
GAMMA_LESS = 0.4
COURANT = 0.4
EPSILON = 1e-06
LANES = 128
ROWS = 8
TINY = 1e-37


def cell_values(density, mom, energy, normal):
    inv = 1.0 / density
    inv_half = 0.5 * inv
    half_vel = [m * inv_half for m in mom]
    kinetic = mom[0] * half_vel[0] + mom[1] * half_vel[1] + mom[2] * half_vel[2]
    pressure = GAMMA_LESS * (energy - kinetic)
    total = energy + pressure
    sound_sq = GAMMA * pressure * inv
    sound = sound_sq * lax.rsqrt(jnp.maximum(sound_sq, TINY))
    half_normal = half_vel[normal]
    flux = [0.5 * mom[normal]]
    for other in range(3):
        part = mom[other] * half_normal
        flux.append(part + 0.5 * pressure if other == normal else part)
    flux.append(total * half_normal)
    means = [half_vel[n] for n in pair_order(normal)] + [total * inv_half]
    return flux, means, jnp.abs(half_normal) + 0.5 * sound


def pair_order(normal):
    return [normal] + [other for other in range(3) if other != normal]


def recon_rest(d1, d2, d3, d4):
    t1 = d2 - d1
    t2 = d3 - d2
    t3 = d4 - d3
    d2s = 0.75 * d2
    d3s = 0.75 * d3
    p2 = d2s * d2 + 0.75 * EPSILON
    p3 = d3s * d3 + 0.75 * EPSILON
    r0 = 1.0 / (t1 * (t1 + d2s) + p2)
    r1 = 1.0 / (t2 * (t2 + d2s) + p2)
    r2 = 1.0 / (t3 * (t3 - d3s) + p3)
    z0 = r0 * r0
    z1 = r1 * r1
    z2 = 1.5 * (r2 * r2)
    num = z0 * (t2 - t1) + z2 * (t3 - t2)
    den = z2 + (0.5 * z0 + 3.0 * z1)
    return num * (1.0 / den)


def central_rest(d_flux):
    return [
        (1.0 / 30.0) * ((d_flux[4][c] - d_flux[0][c]) - 7.0 * (d_flux[3][c] - d_flux[1][c]))
        for c in range(5)
    ]


def face_terms(means):
    a, b, e, h = means
    k = 0.5 * (a * a + b * b + e * e)
    s_sq = GAMMA_LESS * (h - k)
    inv_s = lax.rsqrt(s_sq)
    return [a, b, e, h, k, s_sq * inv_s, (0.5 * GAMMA_LESS) * (inv_s * inv_s), 0.5 * inv_s]


def face_order(normal):
    return [0] + [1 + n for n in pair_order(normal)] + [4]


def weno_waves(d_flux, d_state, terms, alpha, normal):
    order = face_order(normal)
    a, b, e, _, k, _, half_g, half_inv = terms

    def project(x):
        x1 = x[1] - a * x[0]
        x2 = x[2] - b * x[0]
        x3 = x[3] - e * x[0]
        y = half_g * (x[4] - a * x1 - b * x2 - e * x3 - k * x[0])
        z = half_inv * x1
        return [y - z, x[0] - (y + y), x2, x3, y + z]

    up = []
    down = []
    for step in range(5):
        scaled = [alpha * d_state[step][c] for c in order]
        flux = [d_flux[step][c] for c in order]
        up.append([f + q for f, q in zip(flux, scaled)] if step < 4 else None)
        down.append([f - q for f, q in zip(flux, scaled)] if step > 0 else None)
    linear = [(up[1][c] - down[3][c]) - (up[2][c] - down[2][c]) for c in range(5)]
    up = [project(x) if x is not None else None for x in up]
    down = [project(x) if x is not None else None for x in down]
    waves = [
        recon_rest(up[0][c], up[1][c], up[2][c], up[3][c])
        - recon_rest(down[4][c], down[3][c], down[2][c], down[1][c])
        for c in range(5)
    ]
    return linear, waves


def weno_rest(linear, waves, terms, normal):
    a, b, e, h, k, s = terms[:6]
    outer = waves[0] + waves[4]
    shared = outer + waves[1]
    swing = s * (waves[4] - waves[0])
    back = [
        shared,
        a * shared + swing,
        b * shared + waves[2],
        e * shared + waves[3],
        h * outer + k * waves[1] + b * waves[2] + e * waves[3] + a * swing,
    ]
    rest = [None] * 5
    for position, component in enumerate(face_order(normal)):
        rest[component] = (1.0 / 6.0) * (linear[position] - back[position])
    return rest


class Line:
    def __init__(self, refs, normal, unit):
        self.v_ref, self.p_ref, self.w_ref, self.f_ref = refs
        self.normal = normal
        self.unit = unit

    def rows(self, i, off=0):
        start = i * ROWS + off * self.unit
        if (off * self.unit) % ROWS == 0 and not isinstance(i, int):
            start = pl.multiple_of(start, ROWS)
        return pl.ds(start, ROWS)

    def cell(self, i, q):
        n = self.normal
        flux, means, wave = cell_values(q[0], q[1:4], q[4], n)
        now = list(q) + flux + means + [wave]
        here, prev = self.rows(i), self.rows(i, -1)
        for v in range(15):
            self.v_ref[v, here, :] = now[v]
        before = [self.v_ref[v, prev, :] for v in range(15)]
        for v in range(10):
            self.p_ref[v, here, :] = now[v] - before[v]
        self.p_ref[10, here, :] = jnp.maximum(now[14], before[14])
        terms = face_terms([now[v] + before[v] for v in range(10, 14)])
        for v in range(8):
            self.p_ref[11 + v, here, :] = terms[v]

    def pair(self, v, j, off=0):
        return self.p_ref[v, self.rows(j, off), :]

    def fluxes(self, j):
        return [[self.pair(5 + c, j, k - 2) for c in range(5)] for k in range(5)]

    def central(self, j, d_flux):
        for c, value in enumerate(central_rest(d_flux)):
            self.f_ref[c, self.rows(j), :] = value

    def waves(self, j, d_flux):
        d_state = [[self.pair(c, j, k - 2) for c in range(5)] for k in range(5)]
        terms = [self.pair(11 + v, j) for v in range(8)]
        alpha = jnp.maximum(jnp.maximum(self.pair(10, j, -2), self.pair(10, j)), self.pair(10, j, 2))
        linear, waves = weno_waves(d_flux, d_state, terms, alpha, self.normal)
        for c in range(5):
            self.w_ref[c, self.rows(j), :] = linear[c]
            self.w_ref[5 + c, self.rows(j), :] = waves[c]

    def face(self, j):
        both = [self.w_ref[c, self.rows(j), :] for c in range(10)]
        terms = [self.pair(11 + v, j) for v in range(6)]
        for c, value in enumerate(weno_rest(both[:5], both[5:], terms, self.normal)):
            self.f_ref[5 + c, self.rows(j), :] = value

    def change(self, j, first):
        here, following = self.rows(j), self.rows(j, 1)
        return [self.f_ref[first + c, here, :] - self.f_ref[first + c, following, :] for c in range(5)]

    def mean_change(self, j, c):
        return self.pair(5 + c, j) + self.pair(5 + c, j, 1)


def along_lanes(flag_ref, q_ref, out_ref, z_ref, t_ref, v_ref, p_ref, w_ref, f_ref, sems):
    size_x, size_y, width = q_ref.shape[1:]
    q_flat = q_ref.reshape(5, size_x * size_y, width)
    parts = size_x * size_y // LANES
    t_flat = t_ref.reshape(parts * (width // LANES), 5, LANES, LANES)
    groups = width // LANES
    steps = width // ROWS
    blocks = flag_ref.shape[2]
    per_block = steps // blocks
    assert steps & (steps - 1) == 0 and blocks & (blocks - 1) == 0
    line = Line((v_ref, p_ref, w_ref, f_ref), 2, 1)

    def turn_in(part, g):
        lines = pl.ds(pl.multiple_of(part * LANES, LANES), LANES)
        lanes = pl.ds(pl.multiple_of(g * LANES, LANES), LANES)
        for c in range(5):
            z_ref[c, lanes, :] = q_flat[c, lines, lanes].T

    def leave(slot):
        return pltpu.make_async_copy(t_ref.at[slot], out_ref.at[0, slot], sems.at[slot])

    def turn_out(part, g):
        lanes = pl.ds(pl.multiple_of(g * LANES, LANES), LANES)
        slot = part * groups + g
        for c in range(5):
            t_flat[slot, c] = z_ref[5 + c, lanes, :].T
        leave(slot).start()

    def chunk_of(i):
        return (i + (steps - 2)) & (steps - 1)

    def fetch(i):
        at = chunk_of(i)
        rows = pl.ds(pl.multiple_of(at * ROWS, ROWS), ROWS)
        return [z_ref[c, rows, :] for c in range(5)]


    def flag_of(block):
        return flag_ref[0, 0, (block + blocks) & (blocks - 1)]

    def finish(j, flag):
        j = jnp.maximum(j, 0)
        at = jnp.maximum(j - 2, 0)
        rows = pl.ds(pl.multiple_of(at * ROWS, ROWS), ROWS)
        first = jnp.where(flag > 0, 5, 0)
        for c, value in enumerate(line.change(j, first)):
            z_ref[5 + c, rows, :] = value - line.mean_change(j, c)

    def lead(i, carry):
        line.cell(i, fetch(i))
        return carry

    def body(block, carry):
        start = 2 + block * per_block
        own, one, two = flag_of(block), flag_of(block - 1), flag_of(block - 2)
        steps_here = [start + k for k in range(per_block)]

        def lagging():
            finish(start - per_block - 1, two)
            for i in steps_here[:-1]:
                finish(i - per_block, one)

        @pl.when(own + one + two > 0)
        def _():
            for i in steps_here:
                line.face(i - per_block)
            lagging()
            d_flux = [line.fluxes(i) for i in steps_here]
            for i, d in zip(steps_here, d_flux):
                line.waves(i, d)
            for i, d in zip(steps_here, d_flux):
                line.central(i, d)
            for i in steps_here:
                line.cell(i + per_block + 1, fetch(i + per_block + 1))

        @pl.when(own + one + two <= 0)
        def _():
            lagging()
            for i in steps_here:
                line.central(i, line.fluxes(i))
            for i in steps_here:
                line.cell(i + per_block + 1, fetch(i + per_block + 1))

        return carry

    per_group = blocks // groups

    def one_part(part, carry):
        for g in range(groups):
            turn_in(part, g)
        lax.fori_loop(1, 3 + per_block, lead, 0)

        def lane_group(g, carry):
            lax.fori_loop(g * per_group, (g + 1) * per_group, body, 0)

            @pl.when(g > 0)
            def _():
                turn_out(part, g - 1)

            return carry

        lax.fori_loop(0, groups, lane_group, 0)
        for k in range(per_block):
            line.face(steps + 2 - per_block + k)
        for c in range(10):
            f_ref[c, pl.ds(ROWS * (steps + 2), ROWS), :] = f_ref[c, pl.ds(2 * ROWS, ROWS), :]
        for i in range(steps + 1 - per_block, steps + 2):
            finish(i, flag_of((i - 2) // per_block))
        turn_out(part, groups - 1)
        return carry

    lax.fori_loop(0, parts, one_part, 0)
    for slot in range(parts * groups):
        leave(slot).wait()


def along_others(
    flag_ref, top_ref, q_ref, xl_ref, xr_ref, yl_ref, yr_ref, za_ref, zb_ref, adv_ref, ten_ref, v_ref, p_ref, w_ref, f_ref, ty_ref
):
    group = pl.program_id(0)
    size_x, size_y = q_ref.shape[1], q_ref.shape[2]
    q_flat = q_ref.reshape(5, size_x * size_y, LANES)
    ty_flat = ty_ref.reshape(5, size_y * size_x, LANES)
    per_group = flag_ref.shape[2] // pl.num_programs(0)
    edge = LANES // per_group
    lane_block = lax.broadcasted_iota(jnp.int32, (ROWS, LANES), 1) // edge
    marks = jnp.zeros((ROWS, LANES), jnp.int32)
    some = jnp.int32(0)
    for b in range(per_group):
        flag = flag_ref[0, 0, group * per_group + b]
        marks = jnp.where(lane_block == b, flag, marks)
        some = jnp.maximum(some, flag)
    shock = marks > 0

    def march(normal, count, left, middle, right, store):
        line = Line((v_ref, p_ref, w_ref, f_ref), normal, ROWS)

        def from_left(i, carry):
            line.cell(1 + i, left(i))
            return carry

        def from_middle(i, carry):
            line.cell(4 + i, middle(i))
            return carry

        lax.fori_loop(0, 3, from_left, 0, unroll=True)
        lax.fori_loop(0, 4, from_middle, 0, unroll=True)

        def ahead(j):
            inner = j - 1 < count
            near = middle(jnp.minimum(j - 1, count - 1))
            far = right(jnp.clip(j - 1 - count, 0, 2))
            line.cell(j + 3, [jnp.where(inner, n, f) for n, f in zip(near, far)])

        def finish(j, sharp):
            at = jnp.maximum(j - 4, 0)
            change = line.change(j, 0)
            if sharp:
                change = [jnp.where(shock, w, c) for w, c in zip(line.change(j, 5), change)]
            for c in range(5):
                store(at, c, change[c] - line.mean_change(j, c))

        @pl.when(some > 0)
        def _():
            def waves(steps):
                d_flux = [line.fluxes(j) for j in steps]
                for j, d in zip(steps, d_flux):
                    line.waves(j, d)
                for j, d in zip(steps, d_flux):
                    line.central(j, d)

            def two(n, source):
                j = 4 + 2 * n
                for k in (2, 1):
                    line.face(j - k)
                for k in (3, 2):
                    finish(j - k, True)
                waves([j, j + 1])
                for k in (1, 2):
                    line.cell(j + k + 3, source(j + k - 1))
                return 0

            pairs = (count + 1) // 2
            lax.fori_loop(0, pairs - 2, lambda n, _: two(n, middle), 0)
            lax.fori_loop(pairs - 2, pairs, lambda n, _: two(n, lambda i: right(jnp.minimum(i - count, 2))), 0)
            left_over = list(range(4 + 2 * pairs, 5 + count))
            waves(left_over)
            for j in [2 + 2 * pairs, 3 + 2 * pairs] + left_over:
                line.face(j)
            for j in range(1 + 2 * pairs, 4 + count):
                finish(j, True)

        @pl.when(some <= 0)
        def _():
            def body(j, carry):
                ahead(j)
                line.central(j, line.fluxes(j))
                finish(j - 1, False)
                return carry

            lax.fori_loop(4, 5 + count, body, 0)

    def line_x(t, carry):
        rows = pl.ds(pl.multiple_of(t * ROWS, ROWS), ROWS)

        def store(at, c, value):
            ten_ref[c, at, rows, :] = value

        march(
            0,
            size_x,
            lambda i: [xl_ref[c, i, rows, :] for c in range(5)],
            lambda i: [q_ref[c, i, rows, :] for c in range(5)],
            lambda i: [xr_ref[c, i, rows, :] for c in range(5)],
            store,
        )
        return carry

    def line_y(t, carry):
        rows = pl.ds(pl.multiple_of(t * ROWS, ROWS), ROWS)

        def store(at, c, value):
            ty_ref[c, at, rows, :] = value

        march(
            1,
            size_y,
            lambda i: [yl_ref[c, i, rows, :] for c in range(5)],
            lambda i: [q_flat[c, pl.ds(t * (ROWS * size_y) + i, ROWS, stride=size_y), :] for c in range(5)],
            lambda i: [yr_ref[c, i, rows, :] for c in range(5)],
            store,
        )
        return carry

    lax.fori_loop(0, size_y // ROWS, line_x, 0)
    lax.fori_loop(0, size_x // ROWS, line_y, 0)
    step = COURANT / jnp.max(top_ref[...], axis=0, keepdims=True)
    half = size_x // 2

    def last(x, carry):
        for h, part_ref in enumerate((za_ref, zb_ref)):
            for t in range(size_y // ROWS):
                rows = pl.ds(t * ROWS, ROWS)
                for c in range(5):
                    at = h * half + x
                    other = ty_flat[c, pl.ds(t * (ROWS * size_x) + at, ROWS, stride=size_x), :]
                    total = ten_ref[c, at, rows, :] + other + part_ref[c, x, rows, :]
                    ten_ref[c, at, rows, :] = total
                    adv_ref[c, at, rows, :] = q_ref[c, at, rows, :] + step * total
        return carry

    lax.fori_loop(0, half, last, 0)


def prepare(from_ref, xf_ref, xl_ref, yf_ref, yl_ref, top_ref, q_ref, sems):
    size_x, size_y, width = q_ref.shape[1:]

    def speeds(x, top):
        for t in range(size_y // ROWS):
            for g in range(width // LANES):
                q = [q_ref[c, x, pl.ds(t * ROWS, ROWS), pl.ds(g * LANES, LANES)] for c in range(5)]
                inv = 1.0 / q[0]
                kinetic = 0.5 * (q[1] * q[1] + q[2] * q[2] + q[3] * q[3]) * inv
                sound_sq = (GAMMA * GAMMA_LESS) * (q[4] - kinetic) * inv
                sound = sound_sq * lax.rsqrt(jnp.maximum(sound_sq, TINY))
                total = (jnp.abs(q[1]) + jnp.abs(q[2]) + jnp.abs(q[3])) * inv + 3.0 * sound
                top = jnp.maximum(top, total)
        for c in range(5):
            for k in range(3):
                yf_ref[c, k, pl.ds(x, 1), :] = q_ref[c, x, pl.ds(k, 1), :]
                yl_ref[c, k, pl.ds(x, 1), :] = q_ref[c, x, pl.ds(size_y - 3 + k, 1), :]
        return top

    chunks = sems.shape[0]
    per_chunk = size_x // chunks

    def enter(i):
        rows = pl.ds(i * per_chunk, per_chunk)
        return pltpu.make_async_copy(from_ref.at[:, rows], q_ref.at[:, rows], sems.at[i])

    for i in range(chunks):
        enter(i).start()
    top = jnp.zeros((ROWS, LANES), jnp.float32)
    for i in range(chunks):
        enter(i).wait()
        top = lax.fori_loop(i * per_chunk, (i + 1) * per_chunk, speeds, top)
    top_ref[...] = jnp.full(top_ref.shape, jnp.max(top), jnp.float32)
    for c in range(5):
        for k in range(3):
            xf_ref[c, k] = q_ref[c, k]
            xl_ref[c, k] = q_ref[c, size_x - 3 + k]


def line_scratch(rows):
    return [pltpu.VMEM((count, rows, LANES), jnp.float32) for count in (15, 19, 10, 10)]


WHOLE = pl.BlockSpec(memory_space=pltpu.VMEM)
SPARE = 14


def call_prepare(conserved, rows):
    _, size_x, size_y, size_z = conserved.shape
    layers = jax.ShapeDtypeStruct((5, 3, size_y, size_z), jnp.float32)
    turned = jax.ShapeDtypeStruct((5, 3, size_x, size_z), jnp.float32)
    return pl.pallas_call(
        prepare,
        out_shape=[layers, layers, turned, turned, jax.ShapeDtypeStruct((rows, LANES), jnp.float32)],
        in_specs=[pl.BlockSpec(memory_space=pl.ANY)],
        out_specs=[WHOLE] * 5,
        scratch_shapes=[pltpu.VMEM(conserved.shape, jnp.float32), pltpu.SemaphoreType.DMA((4,))],
        cost_estimate=pl.CostEstimate(flops=4_000_000, bytes_accessed=2 * conserved.size * 4, transcendentals=0),
        name="prepare",
    )(conserved)


def call_lanes(flags, conserved):
    _, size_x, size_y, size_z = conserved.shape
    parts = size_x * size_y // LANES
    block = (parts * (size_z // LANES), 5, LANES // size_y, size_y, LANES)
    return pl.pallas_call(
        along_lanes,
        out_shape=jax.ShapeDtypeStruct((SPARE, *block), jnp.float32),
        in_specs=[pl.BlockSpec(memory_space=pltpu.SMEM), WHOLE],
        out_specs=pl.BlockSpec(memory_space=pl.ANY),
        scratch_shapes=[pltpu.VMEM((10, size_z, LANES), jnp.float32), pltpu.VMEM(block, jnp.float32)]
        + line_scratch(size_z + 8 * ROWS)
        + [pltpu.SemaphoreType.DMA((block[0],))],
        cost_estimate=pl.CostEstimate(flops=120_000_000, bytes_accessed=2 * conserved.size * 4, transcendentals=0),
        compiler_params=pltpu.CompilerParams(vmem_limit_bytes=30 << 20),
        name="along_lanes",
    )(flags, conserved)


def call_others(flags, top, conserved, x_low, x_high, y_low, y_high, part):
    _, size_x, size_y, size_z = conserved.shape

    def spec(first, second):
        return pl.BlockSpec((5, first, second, LANES), lambda g: (0, 0, 0, g))

    whole = spec(size_x, size_y)
    groups = size_z // LANES

    def half(h):
        block = (pl.Squeezed(), pl.Squeezed(), 5, size_x // 2, size_y, LANES)
        return pl.BlockSpec(block, lambda g: (0, h * groups + g, 0, 0, 0, 0))

    return pl.pallas_call(
        along_others,
        out_shape=[jax.ShapeDtypeStruct(conserved.shape, jnp.float32)] * 2,
        grid=(size_z // LANES,),
        in_specs=[
            pl.BlockSpec(memory_space=pltpu.SMEM),
            pl.BlockSpec(top.shape, lambda g: (0, 0)),
            whole,
            spec(3, size_y),
            spec(3, size_y),
            spec(3, size_x),
            spec(3, size_x),
            half(0),
            half(1),
        ],
        out_specs=[whole, whole],
        scratch_shapes=line_scratch((max(size_x, size_y) + 9) * ROWS)
        + [pltpu.VMEM((5, size_y, size_x, LANES), jnp.float32)],
        cost_estimate=pl.CostEstimate(flops=240_000_000, bytes_accessed=4 * conserved.size * 4, transcendentals=0),
        compiler_params=pltpu.CompilerParams(vmem_limit_bytes=24 << 20),
        name="along_others",
    )(flags, top, conserved, x_low, x_high, y_low, y_high, part, part)


def neighbours(axis, first, last):
    size = lax.axis_size(axis)
    up = [(i, (i + 1) % size) for i in range(size)]
    down = [(j, i) for i, j in up]
    return lax.ppermute(last, axis, up), lax.ppermute(first, axis, down)


def shards(conserved, shock_flags):
    everyone = ("gx", "gy")
    x_first, x_last, y_first, y_last, top = call_prepare(conserved, lax.axis_size(everyone))
    x_low, x_high = neighbours("gx", x_first, x_last)
    y_low, y_high = neighbours("gy", y_first, y_last)
    top = lax.all_to_all(top, everyone, 0, 0, tiled=True)
    part = call_lanes(shock_flags, conserved)
    return call_others(shock_flags, top, conserved, x_low, x_high, y_low, y_high, part)


def local(conserved, shock_flags, top, x_low, x_high, y_low, y_high):
    x_first, x_last, y_first, y_last, mine = call_prepare(conserved, 256)
    part = call_lanes(shock_flags, conserved)
    return call_others(shock_flags, mine, conserved, x_last, x_first, y_last, y_first, part)


def solution(mesh):
    spec = P(None, "gx", "gy", None)
    return jax.shard_map(
        shards,
        mesh=mesh,
        in_specs=(spec, P("gx", "gy", None)),
        out_specs=(spec, spec),
        check_vma=False,
    )
```

```python
import functools

import jax
import jax.numpy as jnp
from jax import lax
from jax.experimental import pallas as pl
from jax.experimental.pallas import tpu as pltpu
from jax.sharding import PartitionSpec as P

GAMMA = 1.4
GAMMA_LESS = 0.4
COURANT = 0.4
EPSILON = 1e-06
LANES = 128
ROWS = 8
WIDE = 4
TINY = 1e-37


def cell_values(density, mom, energy, normal):
    inv = 1.0 / density
    inv_half = 0.5 * inv
    half_vel = [m * inv_half for m in mom]
    kinetic = mom[0] * half_vel[0] + mom[1] * half_vel[1] + mom[2] * half_vel[2]
    pressure = GAMMA_LESS * (energy - kinetic)
    total = energy + pressure
    sound_sq = GAMMA * pressure * inv
    sound = sound_sq * lax.rsqrt(jnp.maximum(sound_sq, TINY))
    half_normal = half_vel[normal]
    flux = [0.5 * mom[normal]]
    for other in range(3):
        part = mom[other] * half_normal
        flux.append(part + 0.5 * pressure if other == normal else part)
    flux.append(total * half_normal)
    means = [half_vel[n] for n in pair_order(normal)] + [total * inv_half]
    return flux, means, jnp.abs(half_normal) + 0.5 * sound


def pair_order(normal):
    return [normal] + [other for other in range(3) if other != normal]


def recon_rest(d1, d2, d3, d4):
    t1 = d2 - d1
    t2 = d3 - d2
    t3 = d4 - d3
    d2s = 0.75 * d2
    d3s = 0.75 * d3
    p2 = d2s * d2 + 0.75 * EPSILON
    p3 = d3s * d3 + 0.75 * EPSILON
    r0 = 1.0 / (t1 * (t1 + d2s) + p2)
    r1 = 1.0 / (t2 * (t2 + d2s) + p2)
    r2 = 1.0 / (t3 * (t3 - d3s) + p3)
    z0 = r0 * r0
    z1 = r1 * r1
    z2 = 1.5 * (r2 * r2)
    num = z0 * (t2 - t1) + z2 * (t3 - t2)
    den = z2 + (0.5 * z0 + 3.0 * z1)
    return num * (1.0 / den)


def central_rest(d_flux):
    return [
        (1.0 / 30.0) * ((d_flux[4][c] - d_flux[0][c]) - 7.0 * (d_flux[3][c] - d_flux[1][c]))
        for c in range(5)
    ]


def face_terms(means):
    a, b, e, h = means
    k = 0.5 * (a * a + b * b + e * e)
    s_sq = GAMMA_LESS * (h - k)
    inv_s = lax.rsqrt(s_sq)
    return [a, b, e, h, k, s_sq * inv_s, (0.5 * GAMMA_LESS) * (inv_s * inv_s), 0.5 * inv_s]


def face_order(normal):
    return [0] + [1 + n for n in pair_order(normal)] + [4]


def weno_waves(d_flux, d_state, terms, alpha, normal):
    order = face_order(normal)
    a, b, e, _, k, _, half_g, half_inv = terms

    def project(x):
        x1 = x[1] - a * x[0]
        x2 = x[2] - b * x[0]
        x3 = x[3] - e * x[0]
        y = half_g * (x[4] - a * x1 - b * x2 - e * x3 - k * x[0])
        z = half_inv * x1
        return [y - z, x[0] - (y + y), x2, x3, y + z]

    up = []
    down = []
    for step in range(5):
        scaled = [alpha * d_state[step][c] for c in order]
        flux = [d_flux[step][c] for c in order]
        up.append([f + q for f, q in zip(flux, scaled)] if step < 4 else None)
        down.append([f - q for f, q in zip(flux, scaled)] if step > 0 else None)
    linear = [(up[1][c] - down[3][c]) - (up[2][c] - down[2][c]) for c in range(5)]
    up = [project(x) if x is not None else None for x in up]
    down = [project(x) if x is not None else None for x in down]
    waves = [
        recon_rest(up[0][c], up[1][c], up[2][c], up[3][c])
        - recon_rest(down[4][c], down[3][c], down[2][c], down[1][c])
        for c in range(5)
    ]
    return linear, waves


def weno_rest(linear, waves, terms, normal):
    a, b, e, h, k, s = terms[:6]
    outer = waves[0] + waves[4]
    shared = outer + waves[1]
    swing = s * (waves[4] - waves[0])
    back = [
        shared,
        a * shared + swing,
        b * shared + waves[2],
        e * shared + waves[3],
        h * outer + k * waves[1] + b * waves[2] + e * waves[3] + a * swing,
    ]
    rest = [None] * 5
    for position, component in enumerate(face_order(normal)):
        rest[component] = (1.0 / 6.0) * (linear[position] - back[position])
    return rest


class Line:
    def __init__(self, refs, normal, unit):
        self.v_ref, self.p_ref, self.w_ref, self.f_ref = refs
        self.normal = normal
        self.unit = unit

    def rows(self, i, off=0):
        start = i * ROWS + off * self.unit
        if (off * self.unit) % ROWS == 0 and not isinstance(i, int):
            start = pl.multiple_of(start, ROWS)
        return pl.ds(start, ROWS)

    def cell(self, i, q):
        n = self.normal
        flux, means, wave = cell_values(q[0], q[1:4], q[4], n)
        now = list(q) + flux + means + [wave]
        here, prev = self.rows(i), self.rows(i, -1)
        for v in range(15):
            self.v_ref[v, here, :] = now[v]
        before = [self.v_ref[v, prev, :] for v in range(15)]
        for v in range(10):
            self.p_ref[v, here, :] = now[v] - before[v]
        self.p_ref[10, here, :] = jnp.maximum(now[14], before[14])
        terms = face_terms([now[v] + before[v] for v in range(10, 14)])
        for v in range(8):
            self.p_ref[11 + v, here, :] = terms[v]

    def pair(self, v, j, off=0):
        return self.p_ref[v, self.rows(j, off), :]

    def fluxes(self, j):
        return [[self.pair(5 + c, j, k - 2) for c in range(5)] for k in range(5)]

    def central(self, j, d_flux):
        for c, value in enumerate(central_rest(d_flux)):
            self.f_ref[c, self.rows(j), :] = value

    def waves(self, j, d_flux):
        d_state = [[self.pair(c, j, k - 2) for c in range(5)] for k in range(5)]
        terms = [self.pair(11 + v, j) for v in range(8)]
        alpha = jnp.maximum(jnp.maximum(self.pair(10, j, -2), self.pair(10, j)), self.pair(10, j, 2))
        linear, waves = weno_waves(d_flux, d_state, terms, alpha, self.normal)
        for c in range(5):
            self.w_ref[c, self.rows(j), :] = linear[c]
            self.w_ref[5 + c, self.rows(j), :] = waves[c]

    def face(self, j):
        both = [self.w_ref[c, self.rows(j), :] for c in range(10)]
        terms = [self.pair(11 + v, j) for v in range(6)]
        for c, value in enumerate(weno_rest(both[:5], both[5:], terms, self.normal)):
            self.f_ref[5 + c, self.rows(j), :] = value

    def change(self, j, first):
        here, following = self.rows(j), self.rows(j, 1)
        return [self.f_ref[first + c, here, :] - self.f_ref[first + c, following, :] for c in range(5)]

    def mean_change(self, j, c):
        return self.pair(5 + c, j) + self.pair(5 + c, j, 1)


def along_lanes(flag_ref, q_ref, out_ref, z_ref, t_ref, v_ref, p_ref, w_ref, f_ref, sems):
    size_x, size_y, width = q_ref.shape[1:]
    q_flat = q_ref.reshape(5, size_x * size_y, width)
    parts = size_x * size_y // LANES
    t_flat = t_ref.reshape(parts * (width // LANES), 5, LANES, LANES)
    groups = width // LANES
    steps = width // ROWS
    blocks = flag_ref.shape[2]
    per_block = steps // blocks
    assert steps & (steps - 1) == 0 and blocks & (blocks - 1) == 0
    span = 2 * per_block
    line = Line((v_ref, p_ref, w_ref, f_ref), 2, 1)

    def turn_in(part, g):
        lines = pl.ds(pl.multiple_of(part * LANES, LANES), LANES)
        lanes = pl.ds(pl.multiple_of(g * LANES, LANES), LANES)
        for c in range(5):
            z_ref[c, lanes, :] = q_flat[c, lines, lanes].T

    def leave(slot):
        return pltpu.make_async_copy(t_ref.at[slot], out_ref.at[0, slot], sems.at[slot])

    def turn_out(part, g):
        lanes = pl.ds(pl.multiple_of(g * LANES, LANES), LANES)
        slot = part * groups + g
        for c in range(5):
            t_flat[slot, c] = z_ref[5 + c, lanes, :].T
        leave(slot).start()

    def chunk_of(i):
        return (i + (steps - 2)) & (steps - 1)

    def fetch(i):
        at = chunk_of(i)
        rows = pl.ds(pl.multiple_of(at * ROWS, ROWS), ROWS)
        return [z_ref[c, rows, :] for c in range(5)]


    def flag_of(block):
        return flag_ref[0, 0, (block + blocks) & (blocks - 1)]

    def finish(j, flag):
        j = jnp.maximum(j, 0)
        at = jnp.maximum(j - 2, 0)
        rows = pl.ds(pl.multiple_of(at * ROWS, ROWS), ROWS)
        first = jnp.where(flag > 0, 5, 0)
        for c, value in enumerate(line.change(j, first)):
            z_ref[5 + c, rows, :] = value - line.mean_change(j, c)

    def lead(i, carry):
        line.cell(i, fetch(i))
        return carry

    def body(turn, carry):
        start = 2 + turn * span
        first = turn * span // per_block
        flags = {k: flag_of(first + k // per_block) for k in range(-span - 1, span)}
        some = functools.reduce(lambda x, y: x | y, flags.values())
        steps_here = [start + k for k in range(span)]

        def lagging():
            for k in range(-span - 1, -1):
                finish(start + k, flags[k])

        @pl.when(some > 0)
        def _():
            for i in steps_here:
                line.face(jnp.maximum(i - span, 0))
            lagging()
            d_flux = [line.fluxes(i) for i in steps_here]
            for i, d in zip(steps_here, d_flux):
                line.waves(i, d)
            for i, d in zip(steps_here, d_flux):
                line.central(i, d)
            for i in steps_here:
                line.cell(i + span + 1, fetch(i + span + 1))

        @pl.when(some <= 0)
        def _():
            lagging()
            for i in steps_here:
                line.central(i, line.fluxes(i))
            for i in steps_here:
                line.cell(i + span + 1, fetch(i + span + 1))

        return carry

    per_group = steps // groups // span

    def one_part(part, carry):
        for g in range(groups):
            turn_in(part, g)
        lax.fori_loop(1, 3 + span, lead, 0)

        def lane_group(g, carry):
            lax.fori_loop(g * per_group, (g + 1) * per_group, body, 0)

            @pl.when(g > 0)
            def _():
                turn_out(part, g - 1)

            return carry

        lax.fori_loop(0, groups, lane_group, 0)
        for k in range(span):
            line.face(steps + 2 - span + k)
        for c in range(10):
            f_ref[c, pl.ds(ROWS * (steps + 2), ROWS), :] = f_ref[c, pl.ds(2 * ROWS, ROWS), :]
        for i in range(steps + 1 - span, steps + 2):
            finish(i, flag_of((i - 2) // per_block))
        turn_out(part, groups - 1)
        return carry

    lax.fori_loop(0, parts, one_part, 0)
    for slot in range(parts * groups):
        leave(slot).wait()


def along_others(
    flag_ref, top_ref, q_ref, xl_ref, xr_ref, yl_ref, yr_ref, za_ref, zb_ref, adv_ref, ten_ref, v_ref, p_ref, w_ref, f_ref, ty_ref
):
    group = pl.program_id(0)
    size_x, size_y = q_ref.shape[1], q_ref.shape[2]
    q_flat = q_ref.reshape(5, size_x * size_y, LANES)
    ty_flat = ty_ref.reshape(5, size_y * size_x, LANES)
    per_group = flag_ref.shape[2] // pl.num_programs(0)
    edge = LANES // per_group
    lane_block = lax.broadcasted_iota(jnp.int32, (ROWS, LANES), 1) // edge
    marks = jnp.zeros((ROWS, LANES), jnp.int32)
    some = jnp.int32(0)
    for b in range(per_group):
        flag = flag_ref[0, 0, group * per_group + b]
        marks = jnp.where(lane_block == b, flag, marks)
        some = jnp.maximum(some, flag)
    shock = marks > 0

    def march(normal, count, left, middle, right, store):
        line = Line((v_ref, p_ref, w_ref, f_ref), normal, ROWS)

        def from_left(i, carry):
            line.cell(1 + i, left(i))
            return carry

        def from_middle(i, carry):
            line.cell(4 + i, middle(i))
            return carry

        lax.fori_loop(0, 3, from_left, 0, unroll=True)
        lax.fori_loop(0, 2 * WIDE, from_middle, 0, unroll=True)

        def ahead(j):
            inner = j - 1 < count
            near = middle(jnp.minimum(j - 1, count - 1))
            far = right(jnp.clip(j - 1 - count, 0, 2))
            line.cell(j + 3, [jnp.where(inner, n, f) for n, f in zip(near, far)])

        def finish(j, sharp):
            at = jnp.maximum(j - 4, 0)
            change = line.change(j, 0)
            if sharp:
                change = [jnp.where(shock, w, c) for w, c in zip(line.change(j, 5), change)]
            for c in range(5):
                store(at, c, change[c] - line.mean_change(j, c))

        @pl.when(some > 0)
        def _():
            def waves(steps):
                d_flux = [line.fluxes(j) for j in steps]
                for j, d in zip(steps, d_flux):
                    line.waves(j, d)
                for j, d in zip(steps, d_flux):
                    line.central(j, d)

            def stage(j, width, steps_ahead, source):
                for k in range(WIDE, 0, -1):
                    line.face(j - k)
                for k in range(WIDE + 1, 1, -1):
                    finish(jnp.maximum(j - k, 0), True)
                waves([j + k for k in range(width)])
                for i in steps_ahead:
                    line.cell(i, source(i - 4))

            def inner(n, carry):
                j = 4 + WIDE * n
                stage(j, WIDE, [j + 2 * WIDE + k for k in range(WIDE)], middle)
                return carry

            assert count % WIDE == 0
            lax.fori_loop(0, count // WIDE - 2, inner, 0)
            stage(4 + count - 2 * WIDE, WIDE, range(4 + count, 7 + count), lambda i: right(i - count))
            stage(4 + count - WIDE, WIDE + 1, [], None)
            for k in range(WIDE + 1):
                line.face(4 + count - WIDE + k)
            for j in range(3 + count - WIDE, 4 + count):
                finish(j, True)

        @pl.when(some <= 0)
        def _():
            def body(j, carry):
                ahead(j)
                line.central(j, line.fluxes(j))
                finish(j - 1, False)
                return carry

            lax.fori_loop(4, 5 + count, body, 0)

    def line_x(t, carry):
        rows = pl.ds(pl.multiple_of(t * ROWS, ROWS), ROWS)

        def store(at, c, value):
            ten_ref[c, at, rows, :] = value

        march(
            0,
            size_x,
            lambda i: [xl_ref[c, i, rows, :] for c in range(5)],
            lambda i: [q_ref[c, i, rows, :] for c in range(5)],
            lambda i: [xr_ref[c, i, rows, :] for c in range(5)],
            store,
        )
        return carry

    def line_y(t, carry):
        rows = pl.ds(pl.multiple_of(t * ROWS, ROWS), ROWS)

        def store(at, c, value):
            ty_ref[c, at, rows, :] = value

        march(
            1,
            size_y,
            lambda i: [yl_ref[c, i, rows, :] for c in range(5)],
            lambda i: [q_flat[c, pl.ds(t * (ROWS * size_y) + i, ROWS, stride=size_y), :] for c in range(5)],
            lambda i: [yr_ref[c, i, rows, :] for c in range(5)],
            store,
        )
        return carry

    lax.fori_loop(0, size_y // ROWS, line_x, 0)
    lax.fori_loop(0, size_x // ROWS, line_y, 0)
    step = COURANT / jnp.max(top_ref[...], axis=0, keepdims=True)
    half = size_x // 2

    def last(x, carry):
        for h, part_ref in enumerate((za_ref, zb_ref)):
            for t in range(size_y // ROWS):
                rows = pl.ds(t * ROWS, ROWS)
                for c in range(5):
                    at = h * half + x
                    other = ty_flat[c, pl.ds(t * (ROWS * size_x) + at, ROWS, stride=size_x), :]
                    total = ten_ref[c, at, rows, :] + other + part_ref[c, x, rows, :]
                    ten_ref[c, at, rows, :] = total
                    adv_ref[c, at, rows, :] = q_ref[c, at, rows, :] + step * total
        return carry

    lax.fori_loop(0, half, last, 0)


def prepare(from_ref, xf_ref, xl_ref, yf_ref, yl_ref, top_ref, q_ref, sems):
    size_x, size_y, width = q_ref.shape[1:]

    def speeds(x, top):
        for t in range(size_y // ROWS):
            for g in range(width // LANES):
                q = [q_ref[c, x, pl.ds(t * ROWS, ROWS), pl.ds(g * LANES, LANES)] for c in range(5)]
                inv = 1.0 / q[0]
                kinetic = 0.5 * (q[1] * q[1] + q[2] * q[2] + q[3] * q[3]) * inv
                sound_sq = (GAMMA * GAMMA_LESS) * (q[4] - kinetic) * inv
                sound = sound_sq * lax.rsqrt(jnp.maximum(sound_sq, TINY))
                total = (jnp.abs(q[1]) + jnp.abs(q[2]) + jnp.abs(q[3])) * inv + 3.0 * sound
                top = jnp.maximum(top, total)
        for c in range(5):
            for k in range(3):
                yf_ref[c, k, pl.ds(x, 1), :] = q_ref[c, x, pl.ds(k, 1), :]
                yl_ref[c, k, pl.ds(x, 1), :] = q_ref[c, x, pl.ds(size_y - 3 + k, 1), :]
        return top

    chunks = sems.shape[0]
    per_chunk = size_x // chunks

    def enter(i):
        rows = pl.ds(i * per_chunk, per_chunk)
        return pltpu.make_async_copy(from_ref.at[:, rows], q_ref.at[:, rows], sems.at[i])

    for i in range(chunks):
        enter(i).start()
    top = jnp.zeros((ROWS, LANES), jnp.float32)
    for i in range(chunks):
        enter(i).wait()
        top = lax.fori_loop(i * per_chunk, (i + 1) * per_chunk, speeds, top)
    top_ref[...] = jnp.full(top_ref.shape, jnp.max(top), jnp.float32)
    for c in range(5):
        for k in range(3):
            xf_ref[c, k] = q_ref[c, k]
            xl_ref[c, k] = q_ref[c, size_x - 3 + k]


def line_scratch(rows):
    return [pltpu.VMEM((count, rows, LANES), jnp.float32) for count in (15, 19, 10, 10)]


WHOLE = pl.BlockSpec(memory_space=pltpu.VMEM)
SPARE = 14


def call_prepare(conserved, rows):
    _, size_x, size_y, size_z = conserved.shape
    layers = jax.ShapeDtypeStruct((5, 3, size_y, size_z), jnp.float32)
    turned = jax.ShapeDtypeStruct((5, 3, size_x, size_z), jnp.float32)
    return pl.pallas_call(
        prepare,
        out_shape=[layers, layers, turned, turned, jax.ShapeDtypeStruct((rows, LANES), jnp.float32)],
        in_specs=[pl.BlockSpec(memory_space=pl.ANY)],
        out_specs=[WHOLE] * 5,
        scratch_shapes=[pltpu.VMEM(conserved.shape, jnp.float32), pltpu.SemaphoreType.DMA((4,))],
        cost_estimate=pl.CostEstimate(flops=4_000_000, bytes_accessed=2 * conserved.size * 4, transcendentals=0),
        name="prepare",
    )(conserved)


def call_lanes(flags, conserved):
    _, size_x, size_y, size_z = conserved.shape
    parts = size_x * size_y // LANES
    block = (parts * (size_z // LANES), 5, LANES // size_y, size_y, LANES)
    return pl.pallas_call(
        along_lanes,
        out_shape=jax.ShapeDtypeStruct((SPARE, *block), jnp.float32),
        in_specs=[pl.BlockSpec(memory_space=pltpu.SMEM), WHOLE],
        out_specs=pl.BlockSpec(memory_space=pl.ANY),
        scratch_shapes=[pltpu.VMEM((10, size_z, LANES), jnp.float32), pltpu.VMEM(block, jnp.float32)]
        + line_scratch(size_z + 9 * ROWS)
        + [pltpu.SemaphoreType.DMA((block[0],))],
        cost_estimate=pl.CostEstimate(flops=120_000_000, bytes_accessed=2 * conserved.size * 4, transcendentals=0),
        compiler_params=pltpu.CompilerParams(vmem_limit_bytes=30 << 20),
        name="along_lanes",
    )(flags, conserved)


def call_others(flags, top, conserved, x_low, x_high, y_low, y_high, part):
    _, size_x, size_y, size_z = conserved.shape

    def spec(first, second):
        return pl.BlockSpec((5, first, second, LANES), lambda g: (0, 0, 0, g))

    whole = spec(size_x, size_y)
    groups = size_z // LANES

    def half(h):
        block = (pl.Squeezed(), pl.Squeezed(), 5, size_x // 2, size_y, LANES)
        return pl.BlockSpec(block, lambda g: (0, h * groups + g, 0, 0, 0, 0))

    return pl.pallas_call(
        along_others,
        out_shape=[jax.ShapeDtypeStruct(conserved.shape, jnp.float32)] * 2,
        grid=(size_z // LANES,),
        in_specs=[
            pl.BlockSpec(memory_space=pltpu.SMEM),
            pl.BlockSpec(top.shape, lambda g: (0, 0)),
            whole,
            spec(3, size_y),
            spec(3, size_y),
            spec(3, size_x),
            spec(3, size_x),
            half(0),
            half(1),
        ],
        out_specs=[whole, whole],
        scratch_shapes=line_scratch((max(size_x, size_y) + 9) * ROWS)
        + [pltpu.VMEM((5, size_y, size_x, LANES), jnp.float32)],
        cost_estimate=pl.CostEstimate(flops=240_000_000, bytes_accessed=4 * conserved.size * 4, transcendentals=0),
        compiler_params=pltpu.CompilerParams(vmem_limit_bytes=24 << 20),
        name="along_others",
    )(flags, top, conserved, x_low, x_high, y_low, y_high, part, part)


def neighbours(axis, first, last):
    size = lax.axis_size(axis)
    up = [(i, (i + 1) % size) for i in range(size)]
    down = [(j, i) for i, j in up]
    return lax.ppermute(last, axis, up), lax.ppermute(first, axis, down)


def shards(conserved, shock_flags):
    everyone = ("gx", "gy")
    x_first, x_last, y_first, y_last, top = call_prepare(conserved, lax.axis_size(everyone))
    x_low, x_high = neighbours("gx", x_first, x_last)
    y_low, y_high = neighbours("gy", y_first, y_last)
    top = lax.all_to_all(top, everyone, 0, 0, tiled=True)
    part = call_lanes(shock_flags, conserved)
    return call_others(shock_flags, top, conserved, x_low, x_high, y_low, y_high, part)


def local(conserved, shock_flags, top, x_low, x_high, y_low, y_high):
    x_first, x_last, y_first, y_last, mine = call_prepare(conserved, 256)
    part = call_lanes(shock_flags, conserved)
    return call_others(shock_flags, mine, conserved, x_last, x_first, y_last, y_first, part)


def solution(mesh):
    spec = P(None, "gx", "gy", None)
    return jax.shard_map(
        shards,
        mesh=mesh,
        in_specs=(spec, P("gx", "gy", None)),
        out_specs=(spec, spec),
        check_vma=False,
    )
```

```python
import functools

import jax
import jax.numpy as jnp
from jax import lax
from jax.experimental import pallas as pl
from jax.experimental.pallas import tpu as pltpu
from jax.sharding import PartitionSpec as P

GAMMA = 1.4
GAMMA_LESS = 0.4
COURANT = 0.4
EPSILON = 1e-06
LANES = 128
ROWS = 8
WIDE = 4
TINY = 1e-37


def cell_values(density, mom, energy, normal):
    inv = 1.0 / density
    inv_half = 0.5 * inv
    half_vel = [m * inv_half for m in mom]
    kinetic = mom[0] * half_vel[0] + mom[1] * half_vel[1] + mom[2] * half_vel[2]
    pressure = GAMMA_LESS * (energy - kinetic)
    total = energy + pressure
    sound_sq = GAMMA * pressure * inv
    sound = sound_sq * lax.rsqrt(jnp.maximum(sound_sq, TINY))
    half_normal = half_vel[normal]
    flux = [0.5 * mom[normal]]
    for other in range(3):
        part = mom[other] * half_normal
        flux.append(part + 0.5 * pressure if other == normal else part)
    flux.append(total * half_normal)
    means = [half_vel[n] for n in pair_order(normal)] + [total * inv_half]
    return flux, means, jnp.abs(half_normal) + 0.5 * sound


def pair_order(normal):
    return [normal] + [other for other in range(3) if other != normal]


def recon_rest(d1, d2, d3, d4):
    t1 = d2 - d1
    t2 = d3 - d2
    t3 = d4 - d3
    d2s = 0.75 * d2
    d3s = 0.75 * d3
    p2 = d2s * d2 + 0.75 * EPSILON
    p3 = d3s * d3 + 0.75 * EPSILON
    r0 = 1.0 / (t1 * (t1 + d2s) + p2)
    r1 = 1.0 / (t2 * (t2 + d2s) + p2)
    r2 = 1.0 / (t3 * (t3 - d3s) + p3)
    z0 = r0 * r0
    z1 = r1 * r1
    z2 = 1.5 * (r2 * r2)
    num = z0 * (t2 - t1) + z2 * (t3 - t2)
    den = z2 + (0.5 * z0 + 3.0 * z1)
    return num * (1.0 / den)


def central_rest(d_flux):
    return [
        (1.0 / 30.0) * ((d_flux[4][c] - d_flux[0][c]) - 7.0 * (d_flux[3][c] - d_flux[1][c]))
        for c in range(5)
    ]


def face_terms(means):
    a, b, e, h = means
    k = 0.5 * (a * a + b * b + e * e)
    s_sq = GAMMA_LESS * (h - k)
    inv_s = lax.rsqrt(s_sq)
    return [a, b, e, h, k, s_sq * inv_s, (0.5 * GAMMA_LESS) * (inv_s * inv_s), 0.5 * inv_s]


def face_order(normal):
    return [0] + [1 + n for n in pair_order(normal)] + [4]


def weno_waves(d_flux, d_state, terms, alpha, normal):
    order = face_order(normal)
    a, b, e, _, k, _, half_g, half_inv = terms

    def project(x):
        x1 = x[1] - a * x[0]
        x2 = x[2] - b * x[0]
        x3 = x[3] - e * x[0]
        y = half_g * (x[4] - a * x1 - b * x2 - e * x3 - k * x[0])
        z = half_inv * x1
        return [y - z, x[0] - (y + y), x2, x3, y + z]

    up = []
    down = []
    for step in range(5):
        scaled = [alpha * d_state[step][c] for c in order]
        flux = [d_flux[step][c] for c in order]
        up.append([f + q for f, q in zip(flux, scaled)] if step < 4 else None)
        down.append([f - q for f, q in zip(flux, scaled)] if step > 0 else None)
    linear = [(up[1][c] - down[3][c]) - (up[2][c] - down[2][c]) for c in range(5)]
    up = [project(x) if x is not None else None for x in up]
    down = [project(x) if x is not None else None for x in down]
    waves = [
        recon_rest(up[0][c], up[1][c], up[2][c], up[3][c])
        - recon_rest(down[4][c], down[3][c], down[2][c], down[1][c])
        for c in range(5)
    ]
    return linear, waves


def weno_rest(linear, waves, terms, normal):
    a, b, e, h, k, s = terms[:6]
    outer = waves[0] + waves[4]
    shared = outer + waves[1]
    swing = s * (waves[4] - waves[0])
    back = [
        shared,
        a * shared + swing,
        b * shared + waves[2],
        e * shared + waves[3],
        h * outer + k * waves[1] + b * waves[2] + e * waves[3] + a * swing,
    ]
    rest = [None] * 5
    for position, component in enumerate(face_order(normal)):
        rest[component] = (1.0 / 6.0) * (linear[position] - back[position])
    return rest


class Line:
    def __init__(self, refs, normal, unit):
        self.v_ref, self.p_ref, self.w_ref, self.f_ref = refs
        self.normal = normal
        self.unit = unit

    def rows(self, i, off=0):
        start = i * ROWS + off * self.unit
        if (off * self.unit) % ROWS == 0 and not isinstance(i, int):
            start = pl.multiple_of(start, ROWS)
        return pl.ds(start, ROWS)

    def cell(self, i, q):
        n = self.normal
        flux, means, wave = cell_values(q[0], q[1:4], q[4], n)
        now = list(q) + flux + means + [wave]
        here, prev = self.rows(i), self.rows(i, -1)
        for v in range(15):
            self.v_ref[v, here, :] = now[v]
        before = [self.v_ref[v, prev, :] for v in range(15)]
        for v in range(10):
            self.p_ref[v, here, :] = now[v] - before[v]
        self.p_ref[10, here, :] = jnp.maximum(now[14], before[14])
        terms = face_terms([now[v] + before[v] for v in range(10, 14)])
        for v in range(8):
            self.p_ref[11 + v, here, :] = terms[v]

    def pair(self, v, j, off=0):
        return self.p_ref[v, self.rows(j, off), :]

    def fluxes(self, j):
        return [[self.pair(5 + c, j, k - 2) for c in range(5)] for k in range(5)]

    def central(self, j, d_flux):
        for c, value in enumerate(central_rest(d_flux)):
            self.f_ref[c, self.rows(j), :] = value

    def waves(self, j, d_flux):
        d_state = [[self.pair(c, j, k - 2) for c in range(5)] for k in range(5)]
        terms = [self.pair(11 + v, j) for v in range(8)]
        alpha = jnp.maximum(jnp.maximum(self.pair(10, j, -2), self.pair(10, j)), self.pair(10, j, 2))
        linear, waves = weno_waves(d_flux, d_state, terms, alpha, self.normal)
        for c in range(5):
            self.w_ref[c, self.rows(j), :] = linear[c]
            self.w_ref[5 + c, self.rows(j), :] = waves[c]

    def face(self, j):
        both = [self.w_ref[c, self.rows(j), :] for c in range(10)]
        terms = [self.pair(11 + v, j) for v in range(6)]
        for c, value in enumerate(weno_rest(both[:5], both[5:], terms, self.normal)):
            self.f_ref[5 + c, self.rows(j), :] = value

    def change(self, j, first):
        here, following = self.rows(j), self.rows(j, 1)
        return [self.f_ref[first + c, here, :] - self.f_ref[first + c, following, :] for c in range(5)]

    def mean_change(self, j, c):
        return self.pair(5 + c, j) + self.pair(5 + c, j, 1)


def along_lanes(flag_ref, q_ref, out_ref, z_ref, t_ref, v_ref, p_ref, w_ref, f_ref, sems):
    size_x, size_y, width = q_ref.shape[1:]
    q_flat = q_ref.reshape(5, size_x * size_y, width)
    parts = size_x * size_y // LANES
    t_flat = t_ref.reshape(parts * (width // LANES), 5, LANES, LANES)
    groups = width // LANES
    steps = width // ROWS
    blocks = flag_ref.shape[2]
    per_block = steps // blocks
    assert steps & (steps - 1) == 0 and blocks & (blocks - 1) == 0
    span = 2 * per_block
    line = Line((v_ref, p_ref, w_ref, f_ref), 2, 1)

    def turn_in(part, g):
        lines = pl.ds(pl.multiple_of(part * LANES, LANES), LANES)
        lanes = pl.ds(pl.multiple_of(g * LANES, LANES), LANES)
        for c in range(5):
            z_ref[c, lanes, :] = q_flat[c, lines, lanes].T

    def leave(slot):
        return pltpu.make_async_copy(t_ref.at[slot], out_ref.at[0, slot], sems.at[slot])

    def turn_out(part, g):
        lanes = pl.ds(pl.multiple_of(g * LANES, LANES), LANES)
        slot = part * groups + g
        for c in range(5):
            t_flat[slot, c] = z_ref[5 + c, lanes, :].T
        leave(slot).start()

    def chunk_of(i):
        return (i + (steps - 2)) & (steps - 1)

    def fetch(i):
        at = chunk_of(i)
        rows = pl.ds(pl.multiple_of(at * ROWS, ROWS), ROWS)
        return [z_ref[c, rows, :] for c in range(5)]


    def flag_of(block):
        return flag_ref[0, 0, (block + blocks) & (blocks - 1)]

    def finish(j, flag):
        j = jnp.maximum(j, 0)
        at = jnp.maximum(j - 2, 0)
        rows = pl.ds(pl.multiple_of(at * ROWS, ROWS), ROWS)
        first = jnp.where(flag > 0, 5, 0)
        for c, value in enumerate(line.change(j, first)):
            z_ref[5 + c, rows, :] = value - line.mean_change(j, c)

    def lead(i, carry):
        line.cell(i, fetch(i))
        return carry

    def body(turn, carry):
        start = 2 + turn * span
        first = turn * span // per_block
        flags = {k: flag_of(first + k // per_block) for k in range(-span - 1, span)}
        some = functools.reduce(lambda x, y: x | y, flags.values())
        steps_here = [start + k for k in range(span)]

        def lagging():
            for k in range(-span - 1, -1):
                finish(start + k, flags[k])

        @pl.when(some > 0)
        def _():
            for i in steps_here:
                line.face(jnp.maximum(i - span, 0))
            lagging()
            d_flux = [line.fluxes(i) for i in steps_here]
            for i, d in zip(steps_here, d_flux):
                line.waves(i, d)
            for i, d in zip(steps_here, d_flux):
                line.central(i, d)
            for i in steps_here:
                line.cell(i + span + 1, fetch(i + span + 1))

        @pl.when(some <= 0)
        def _():
            lagging()
            for i in steps_here:
                line.central(i, line.fluxes(i))
            for i in steps_here:
                line.cell(i + span + 1, fetch(i + span + 1))

        return carry

    def one_part(part, carry):
        for g in range(groups):
            turn_in(part, g)
        lax.fori_loop(1, 3 + span, lead, 0)

        lax.fori_loop(0, steps // span, body, 0)
        for k in range(span):
            line.face(steps + 2 - span + k)
        for c in range(10):
            f_ref[c, pl.ds(ROWS * (steps + 2), ROWS), :] = f_ref[c, pl.ds(2 * ROWS, ROWS), :]
        for i in range(steps + 1 - span, steps + 2):
            finish(i, flag_of((i - 2) // per_block))
        for g in range(groups):
            turn_out(part, g)
        return carry

    lax.fori_loop(0, parts, one_part, 0)
    for slot in range(parts * groups):
        leave(slot).wait()


def along_others(
    flag_ref, top_ref, q_ref, xl_ref, xr_ref, yl_ref, yr_ref, za_ref, zb_ref, adv_ref, ten_ref, v_ref, p_ref, w_ref, f_ref, ty_ref
):
    group = pl.program_id(0)
    size_x, size_y = q_ref.shape[1], q_ref.shape[2]
    q_flat = q_ref.reshape(5, size_x * size_y, LANES)
    ty_flat = ty_ref.reshape(5, size_y * size_x, LANES)
    per_group = flag_ref.shape[2] // pl.num_programs(0)
    edge = LANES // per_group
    lane_block = lax.broadcasted_iota(jnp.int32, (ROWS, LANES), 1) // edge
    marks = jnp.zeros((ROWS, LANES), jnp.int32)
    some = jnp.int32(0)
    for b in range(per_group):
        flag = flag_ref[0, 0, group * per_group + b]
        marks = jnp.where(lane_block == b, flag, marks)
        some = jnp.maximum(some, flag)
    shock = marks > 0

    def march(normal, count, left, middle, right, store):
        line = Line((v_ref, p_ref, w_ref, f_ref), normal, ROWS)

        def from_left(i, carry):
            line.cell(1 + i, left(i))
            return carry

        def from_middle(i, carry):
            line.cell(4 + i, middle(i))
            return carry

        lax.fori_loop(0, 3, from_left, 0, unroll=True)
        lax.fori_loop(0, 2 * WIDE, from_middle, 0, unroll=True)

        def ahead(j):
            inner = j - 1 < count
            near = middle(jnp.minimum(j - 1, count - 1))
            far = right(jnp.clip(j - 1 - count, 0, 2))
            line.cell(j + 3, [jnp.where(inner, n, f) for n, f in zip(near, far)])

        def finish(j, sharp):
            at = jnp.maximum(j - 4, 0)
            change = line.change(j, 0)
            if sharp:
                change = [jnp.where(shock, w, c) for w, c in zip(line.change(j, 5), change)]
            for c in range(5):
                store(at, c, change[c] - line.mean_change(j, c))

        @pl.when(some > 0)
        def _():
            def waves(steps):
                d_flux = [line.fluxes(j) for j in steps]
                for j, d in zip(steps, d_flux):
                    line.waves(j, d)
                for j, d in zip(steps, d_flux):
                    line.central(j, d)

            def stage(j, width, steps_ahead, source):
                for k in range(WIDE, 0, -1):
                    line.face(j - k)
                for k in range(WIDE + 1, 1, -1):
                    finish(jnp.maximum(j - k, 0), True)
                waves([j + k for k in range(width)])
                for i in steps_ahead:
                    line.cell(i, source(i - 4))

            def inner(n, carry):
                j = 4 + WIDE * n
                stage(j, WIDE, [j + 2 * WIDE + k for k in range(WIDE)], middle)
                return carry

            assert count % WIDE == 0
            lax.fori_loop(0, count // WIDE - 2, inner, 0)
            stage(4 + count - 2 * WIDE, WIDE, range(4 + count, 7 + count), lambda i: right(i - count))
            stage(4 + count - WIDE, WIDE + 1, [], None)
            for k in range(WIDE + 1):
                line.face(4 + count - WIDE + k)
            for j in range(3 + count - WIDE, 4 + count):
                finish(j, True)

        @pl.when(some <= 0)
        def _():
            def body(j, carry):
                ahead(j)
                line.central(j, line.fluxes(j))
                finish(j - 1, False)
                return carry

            lax.fori_loop(4, 5 + count, body, 0)

    def line_x(t, carry):
        rows = pl.ds(pl.multiple_of(t * ROWS, ROWS), ROWS)

        def store(at, c, value):
            ten_ref[c, at, rows, :] = value

        march(
            0,
            size_x,
            lambda i: [xl_ref[c, i, rows, :] for c in range(5)],
            lambda i: [q_ref[c, i, rows, :] for c in range(5)],
            lambda i: [xr_ref[c, i, rows, :] for c in range(5)],
            store,
        )
        return carry

    def line_y(t, carry):
        rows = pl.ds(pl.multiple_of(t * ROWS, ROWS), ROWS)

        def store(at, c, value):
            ty_ref[c, at, rows, :] = value

        march(
            1,
            size_y,
            lambda i: [yl_ref[c, i, rows, :] for c in range(5)],
            lambda i: [q_flat[c, pl.ds(t * (ROWS * size_y) + i, ROWS, stride=size_y), :] for c in range(5)],
            lambda i: [yr_ref[c, i, rows, :] for c in range(5)],
            store,
        )
        return carry

    lax.fori_loop(0, size_y // ROWS, line_x, 0)
    lax.fori_loop(0, size_x // ROWS, line_y, 0)
    step = COURANT / jnp.max(top_ref[...], axis=0, keepdims=True)
    half = size_x // 2

    def last(x, carry):
        for h, part_ref in enumerate((za_ref, zb_ref)):
            for t in range(size_y // ROWS):
                rows = pl.ds(t * ROWS, ROWS)
                for c in range(5):
                    at = h * half + x
                    other = ty_flat[c, pl.ds(t * (ROWS * size_x) + at, ROWS, stride=size_x), :]
                    total = ten_ref[c, at, rows, :] + other + part_ref[c, x, rows, :]
                    ten_ref[c, at, rows, :] = total
                    adv_ref[c, at, rows, :] = q_ref[c, at, rows, :] + step * total
        return carry

    lax.fori_loop(0, half, last, 0)


def prepare(from_ref, xf_ref, xl_ref, yf_ref, yl_ref, top_ref, q_ref, sems):
    size_x, size_y, width = q_ref.shape[1:]

    def speeds(x, top):
        for t in range(size_y // ROWS):
            for g in range(width // LANES):
                q = [q_ref[c, x, pl.ds(t * ROWS, ROWS), pl.ds(g * LANES, LANES)] for c in range(5)]
                inv = 1.0 / q[0]
                kinetic = 0.5 * (q[1] * q[1] + q[2] * q[2] + q[3] * q[3]) * inv
                sound_sq = (GAMMA * GAMMA_LESS) * (q[4] - kinetic) * inv
                sound = sound_sq * lax.rsqrt(jnp.maximum(sound_sq, TINY))
                total = (jnp.abs(q[1]) + jnp.abs(q[2]) + jnp.abs(q[3])) * inv + 3.0 * sound
                top = jnp.maximum(top, total)
        for c in range(5):
            for k in range(3):
                yf_ref[c, k, pl.ds(x, 1), :] = q_ref[c, x, pl.ds(k, 1), :]
                yl_ref[c, k, pl.ds(x, 1), :] = q_ref[c, x, pl.ds(size_y - 3 + k, 1), :]
        return top

    chunks = sems.shape[0]
    per_chunk = size_x // chunks

    def enter(i):
        rows = pl.ds(i * per_chunk, per_chunk)
        return pltpu.make_async_copy(from_ref.at[:, rows], q_ref.at[:, rows], sems.at[i])

    for i in range(chunks):
        enter(i).start()
    top = jnp.zeros((ROWS, LANES), jnp.float32)
    for i in range(chunks):
        enter(i).wait()
        top = lax.fori_loop(i * per_chunk, (i + 1) * per_chunk, speeds, top)
    top_ref[...] = jnp.full(top_ref.shape, jnp.max(top), jnp.float32)
    for c in range(5):
        for k in range(3):
            xf_ref[c, k] = q_ref[c, k]
            xl_ref[c, k] = q_ref[c, size_x - 3 + k]


def line_scratch(rows):
    return [pltpu.VMEM((count, rows, LANES), jnp.float32) for count in (15, 19, 10, 10)]


WHOLE = pl.BlockSpec(memory_space=pltpu.VMEM)
SPARE = 14


def call_prepare(conserved, rows):
    _, size_x, size_y, size_z = conserved.shape
    layers = jax.ShapeDtypeStruct((5, 3, size_y, size_z), jnp.float32)
    turned = jax.ShapeDtypeStruct((5, 3, size_x, size_z), jnp.float32)
    return pl.pallas_call(
        prepare,
        out_shape=[layers, layers, turned, turned, jax.ShapeDtypeStruct((rows, LANES), jnp.float32)],
        in_specs=[pl.BlockSpec(memory_space=pl.ANY)],
        out_specs=[WHOLE] * 5,
        scratch_shapes=[pltpu.VMEM(conserved.shape, jnp.float32), pltpu.SemaphoreType.DMA((4,))],
        cost_estimate=pl.CostEstimate(flops=4_000_000, bytes_accessed=2 * conserved.size * 4, transcendentals=0),
        name="prepare",
    )(conserved)


def call_lanes(flags, conserved):
    _, size_x, size_y, size_z = conserved.shape
    parts = size_x * size_y // LANES
    block = (parts * (size_z // LANES), 5, LANES // size_y, size_y, LANES)
    return pl.pallas_call(
        along_lanes,
        out_shape=jax.ShapeDtypeStruct((SPARE, *block), jnp.float32),
        in_specs=[pl.BlockSpec(memory_space=pltpu.SMEM), WHOLE],
        out_specs=pl.BlockSpec(memory_space=pl.ANY),
        scratch_shapes=[pltpu.VMEM((10, size_z, LANES), jnp.float32), pltpu.VMEM(block, jnp.float32)]
        + line_scratch(size_z + 9 * ROWS)
        + [pltpu.SemaphoreType.DMA((block[0],))],
        cost_estimate=pl.CostEstimate(flops=120_000_000, bytes_accessed=2 * conserved.size * 4, transcendentals=0),
        compiler_params=pltpu.CompilerParams(vmem_limit_bytes=30 << 20),
        name="along_lanes",
    )(flags, conserved)


def call_others(flags, top, conserved, x_low, x_high, y_low, y_high, part):
    _, size_x, size_y, size_z = conserved.shape

    def spec(first, second):
        return pl.BlockSpec((5, first, second, LANES), lambda g: (0, 0, 0, g))

    whole = spec(size_x, size_y)
    groups = size_z // LANES

    def half(h):
        block = (pl.Squeezed(), pl.Squeezed(), 5, size_x // 2, size_y, LANES)
        return pl.BlockSpec(block, lambda g: (0, h * groups + g, 0, 0, 0, 0))

    return pl.pallas_call(
        along_others,
        out_shape=[jax.ShapeDtypeStruct(conserved.shape, jnp.float32)] * 2,
        grid=(size_z // LANES,),
        in_specs=[
            pl.BlockSpec(memory_space=pltpu.SMEM),
            pl.BlockSpec(top.shape, lambda g: (0, 0)),
            whole,
            spec(3, size_y),
            spec(3, size_y),
            spec(3, size_x),
            spec(3, size_x),
            half(0),
            half(1),
        ],
        out_specs=[whole, whole],
        scratch_shapes=line_scratch((max(size_x, size_y) + 9) * ROWS)
        + [pltpu.VMEM((5, size_y, size_x, LANES), jnp.float32)],
        cost_estimate=pl.CostEstimate(flops=240_000_000, bytes_accessed=4 * conserved.size * 4, transcendentals=0),
        compiler_params=pltpu.CompilerParams(vmem_limit_bytes=24 << 20),
        name="along_others",
    )(flags, top, conserved, x_low, x_high, y_low, y_high, part, part)


def neighbours(axis, first, last):
    size = lax.axis_size(axis)
    up = [(i, (i + 1) % size) for i in range(size)]
    down = [(j, i) for i, j in up]
    return lax.ppermute(last, axis, up), lax.ppermute(first, axis, down)


def shards(conserved, shock_flags):
    everyone = ("gx", "gy")
    x_first, x_last, y_first, y_last, top = call_prepare(conserved, lax.axis_size(everyone))
    x_low, x_high = neighbours("gx", x_first, x_last)
    y_low, y_high = neighbours("gy", y_first, y_last)
    top = lax.all_to_all(top, everyone, 0, 0, tiled=True)
    part = call_lanes(shock_flags, conserved)
    return call_others(shock_flags, top, conserved, x_low, x_high, y_low, y_high, part)


def local(conserved, shock_flags, top, x_low, x_high, y_low, y_high):
    x_first, x_last, y_first, y_last, mine = call_prepare(conserved, 256)
    part = call_lanes(shock_flags, conserved)
    return call_others(shock_flags, mine, conserved, x_last, x_first, y_last, y_first, part)


def solution(mesh):
    spec = P(None, "gx", "gy", None)
    return jax.shard_map(
        shards,
        mesh=mesh,
        in_specs=(spec, P("gx", "gy", None)),
        out_specs=(spec, spec),
        check_vma=False,
    )
```
